256 devices in a mesh: seq: 32 (over y_hi, z, core), head: 8 (over y_lo, x).
Axes of the slice: x: 4, y: 4 (y_hi: 2, y_lo: 2; y = y_hi * 2 + y_lo), z: 8, core: 2. Of those that a mesh axis runs over, the one named last changes fastest.
Arguments:
- q_cells: bfloat16 [8192, 8192], P('seq', 'head'), may hold values from -60 to 60
- k_cells: bfloat16 [8192, 1024], P('seq', 'head'), may hold values from -11 to 11
- v_cells: bfloat16 [8192, 1024], P('seq', 'head'), may hold values from -6 to 6
- do_cells: bfloat16 [8192, 8192], P('seq', 'head'), may hold values from -6 to 6
- q_head: bfloat16 [1024, 8192], P('seq', 'head'), may hold values from -60 to 60
- k_head: bfloat16 [1024, 1024], P('seq', 'head'), may hold values from -6 to 6
- v_head: bfloat16 [1024, 1024], P('seq', 'head'), may hold values from -6 to 6
- do_head: bfloat16 [1024, 8192], P('seq', 'head'), may hold values from -6 to 6
- vis_mask: int32 [64, 8], P('seq'), may hold values from 0 to 1, as said below
Outputs:
- dq_cells: bfloat16 [8192, 8192], P('seq', 'head')
- dk_cells: bfloat16 [8192, 1024], P('seq', 'head')
- dv_cells: bfloat16 [8192, 1024], P('seq', 'head')
- dq_head: bfloat16 [1024, 8192], P('seq', 'head')
- dk_head: bfloat16 [1024, 1024], P('seq', 'head')
- dv_head: bfloat16 [1024, 1024], P('seq', 'head')
The draws below stay inside these ranges and needn't reach their ends.
Inputs may be any that keep to these rules, and one draw needn't show every extreme that they name: vis_mask[b, t] = 1 lets the cells of block b see the headers of block t.
All inputs are finite; a program needn't handle non-finite values.
Results may differ from the reference program's by a relative error of at most 0.012.
Values may be sent and summed in bfloat16 or wider, within the bound.
A program may use at most 64 MiB of HBM per device.

```python
from functools import partial
import jax
import jax.numpy as jnp
from jax import lax

QH = 64
KVH = 8
HD = 128
W = 256
BLOCK = 128
CELLS = 8192
H = 1024


def basis_of(key, count, width, salt):
    return jnp.clip(jax.random.normal(jax.random.fold_in(key, salt), (count, width), jnp.float32), -6.0, 6.0)


def cell_scale():
    return 0.6 + 1.2 * jnp.arange(CELLS).astype(jnp.float32) / CELLS


def drawn_queries(count, salt, key, factor):
    drawn = jnp.clip(basis_of(key, count, QH * HD, salt) * factor[:, None], -60.0, 60.0)
    return drawn


def draw_k_cells(key, part):
    basis = basis_of(key, CELLS, KVH * HD, 101)
    return (basis * cell_scale()[:, None]).astype(jnp.bfloat16)


def draw_q_cells(key, part):
    return drawn_queries(CELLS, 103, key, jnp.ones((CELLS,), jnp.float32)).astype(jnp.bfloat16)


def draw_k_head(key, part):
    basis = basis_of(key, H, KVH * HD, 111)
    return basis.astype(jnp.bfloat16)


def draw_q_head(key, part):
    lifted = jax.random.randint(jax.random.fold_in(key, 117), (H,), 0, 8) == 0
    factor = jnp.where(lifted, 30.0, 1.0).astype(jnp.float32)
    return drawn_queries(H, 113, key, factor).astype(jnp.bfloat16)


def draw_vis_mask(key, part):
    cell_blocks = CELLS // BLOCK
    head_blocks = H // BLOCK
    position = jnp.arange(cell_blocks)
    visible_level = jnp.minimum(1 + 3 * position // cell_blocks + jax.random.randint(jax.random.fold_in(key, 201), (cell_blocks,), 0, 2), 4)
    dice_rolls = jax.random.randint(jax.random.fold_in(key, 202), (cell_blocks, head_blocks), 0, 4)
    return (dice_rolls < visible_level[:, None]).astype(jnp.int32)


def level_of(rng, dims, split, low, top_value):
    loudness, own = 1.0, jax.random.fold_in(rng, 6)
    for dim, parts in split:
        heights = jnp.exp(jax.random.uniform(jax.random.fold_in(own, dim), (parts,), jnp.float32, low / len(split), top_value / len(split)))
        loudness = loudness * jnp.repeat(heights, dims[dim] // parts).reshape([-1 if axis == dim else 1 for axis in range(len(dims))])
    return loudness


def gaussian(stream_key, extent, scale, reach, cuts=(), kind=jnp.bfloat16):
    drawn = scale * jax.random.normal(stream_key, extent, jnp.float32)
    if cuts:
        drawn = drawn * level_of(stream_key, extent, cuts, -0.22, 0.18)
    return jnp.clip(drawn, -reach, reach).astype(kind)


def setup_inputs(seed: int = 0) -> dict:
    arg_keys = jax.random.split(jax.random.key(seed), 10)
    return {
        "q_cells": draw_q_cells(jax.random.fold_in(arg_keys[9], 71), 0),
        "k_cells": draw_k_cells(jax.random.fold_in(arg_keys[9], 71), 0),
        "v_cells": gaussian(arg_keys[2], (CELLS, KVH * HD), 1.0, 6.0, ((0, 32), (1, 8))),
        "do_cells": gaussian(arg_keys[3], (CELLS, QH * HD), 1.0, 6.0, ((0, 32), (1, 8))),
        "q_head": draw_q_head(jax.random.fold_in(arg_keys[9], 71), 0),
        "k_head": draw_k_head(jax.random.fold_in(arg_keys[9], 71), 0),
        "v_head": gaussian(arg_keys[6], (H, KVH * HD), 1.0, 6.0, ((0, 32), (1, 8))),
        "do_head": gaussian(arg_keys[7], (H, QH * HD), 1.0, 6.0, ((0, 32), (1, 8))),
        "vis_mask": draw_vis_mask(jax.random.fold_in(arg_keys[9], 71), 0),
    }


masked_score = -1.0e30


def product(pattern, former, latter):
    return jnp.einsum(pattern, former.astype(jnp.float32), latter.astype(jnp.float32))


def rounded(values):
    return lax.optimization_barrier(values.astype(jnp.bfloat16)).astype(jnp.float32)


def block_stats(queries, key_rows, visible, scaling):
    scores = product("nkgd,mkd->kgnm", queries, key_rows) * scaling
    kept_scores = jnp.where(visible, scores, masked_score)
    highest = jnp.max(kept_scores, axis=-1)
    totals = jnp.sum(jnp.where(visible, jnp.exp(scores - highest[..., None]), 0.0), axis=-1)
    return highest, totals


def merge_stats(former, latter):
    highest = jnp.maximum(former[0], latter[0])
    return highest, former[1] * jnp.exp(former[0] - highest) + latter[1] * jnp.exp(latter[0] - highest)


def weights_of(queries, key_rows, log_totals, visible, scaling):
    scores = product("nkgd,mkd->kgnm", queries, key_rows) * scaling
    return jnp.where(visible, jnp.exp(scores - log_totals[..., None]), 0.0)


def block_delta(queries, grads_out, key_rows, value_rows, log_totals, visible, scaling):
    weights = weights_of(queries, key_rows, log_totals, visible, scaling)
    slopes = product("nkgd,mkd->kgnm", grads_out, value_rows)
    return jnp.sum(weights * slopes, axis=-1)


def block_grads(queries, grads_out, key_rows, value_rows, log_totals, deltas, visible, scaling):
    weights = weights_of(queries, key_rows, log_totals, visible, scaling)
    slopes = product("nkgd,mkd->kgnm", grads_out, value_rows)
    score_grads = weights * (slopes - deltas[..., None])
    weight_low = rounded(weights)
    grad_low = rounded(score_grads)
    grad_values = product("kgnm,nkgd->mkd", weight_low, grads_out)
    grad_keys = product("kgnm,nkgd->mkd", grad_low, queries) * scaling
    grad_queries = product("kgnm,mkd->nkgd", grad_low, key_rows) * scaling
    return grad_queries, grad_keys, grad_values


def to_rows(values):
    return jnp.transpose(values, (1, 2, 0, 3)).reshape(values.shape[1], values.shape[2], -1)


def from_rows(values, pieces):
    return jnp.transpose(values.reshape(values.shape[0], values.shape[1], pieces, -1), (2, 0, 1, 3))


def reference(q_cells, k_cells, v_cells, do_cells, q_head, k_head, v_head, do_head, vis_mask):
    groups = QH // KVH
    scaling = HD ** -0.5
    regions = CELLS // W
    visible = jnp.repeat(jnp.repeat(vis_mask > 0, BLOCK, axis=0), BLOCK, axis=1)

    def query_stack(array, count):
        return jnp.moveaxis(array.reshape(count, KVH, groups, HD), 1, 0)[:, :, None]

    def key_stack(array, count):
        return jnp.moveaxis(array.reshape(count, KVH, HD), 1, 0)[:, :, None]

    def one_group(operands):
        cell_query, cell_key, cell_value, cell_grad, head_query, head_key, head_value, head_grad = operands
        region_query = cell_query.reshape(regions, W, 1, groups, HD)
        region_grad = cell_grad.reshape(regions, W, 1, groups, HD)
        region_key = cell_key.reshape(regions, W, 1, HD)
        region_value = cell_value.reshape(regions, W, 1, HD)
        local_stats = jax.vmap(partial(block_stats, visible=True, scaling=scaling))(region_query, region_key)
        outer_stats = block_stats(cell_query, head_key, visible, scaling)
        highest, totals = merge_stats((to_rows(local_stats[0]), to_rows(local_stats[1])), outer_stats)
        cell_log = highest + jnp.log(totals)
        region_log = from_rows(cell_log, regions)
        local_delta = to_rows(jax.vmap(partial(block_delta, visible=True, scaling=scaling))(
            region_query, region_grad, region_key, region_value, region_log))
        cell_delta = local_delta + block_delta(cell_query, cell_grad, head_key, head_value, cell_log, visible, scaling)
        local_grads = jax.vmap(partial(block_grads, visible=True, scaling=scaling))(
            region_query, region_grad, region_key, region_value, region_log, from_rows(cell_delta, regions))
        outer_grads = block_grads(cell_query, cell_grad, head_key, head_value, cell_log, cell_delta, visible, scaling)
        head_stats = merge_stats(block_stats(head_query, cell_key, True, scaling),
                                 block_stats(head_query, head_key, True, scaling))
        head_log = head_stats[0] + jnp.log(head_stats[1])
        head_delta = (block_delta(head_query, head_grad, cell_key, cell_value, head_log, True, scaling)
                      + block_delta(head_query, head_grad, head_key, head_value, head_log, True, scaling))
        cross_grads = block_grads(head_query, head_grad, cell_key, cell_value, head_log, head_delta, True, scaling)
        self_grads = block_grads(head_query, head_grad, head_key, head_value, head_log, head_delta, True, scaling)
        grad_cell_query = local_grads[0].reshape(CELLS, 1, groups, HD) + outer_grads[0]
        grad_cell_key = local_grads[1].reshape(CELLS, 1, HD) + cross_grads[1]
        grad_cell_value = local_grads[2].reshape(CELLS, 1, HD) + cross_grads[2]
        grad_head_query = cross_grads[0] + self_grads[0]
        grad_head_key = outer_grads[1] + self_grads[1]
        grad_head_value = outer_grads[2] + self_grads[2]
        return (grad_cell_query.astype(jnp.bfloat16), grad_cell_key.astype(jnp.bfloat16),
                grad_cell_value.astype(jnp.bfloat16), grad_head_query.astype(jnp.bfloat16),
                grad_head_key.astype(jnp.bfloat16), grad_head_value.astype(jnp.bfloat16))

    results = lax.map(one_group, (query_stack(q_cells, CELLS), key_stack(k_cells, CELLS), key_stack(v_cells, CELLS),
                                  query_stack(do_cells, CELLS), query_stack(q_head, H), key_stack(k_head, H),
                                  key_stack(v_head, H), query_stack(do_head, H)))

    def unstack_queries(array, count):
        return jnp.moveaxis(array[:, :, 0], 0, 1).reshape(count, QH * HD)

    def unstack_keys(array, count):
        return jnp.moveaxis(array[:, :, 0], 0, 1).reshape(count, KVH * HD)

    return (unstack_queries(results[0], CELLS), unstack_keys(results[1], CELLS), unstack_keys(results[2], CELLS),
            unstack_queries(results[3], H), unstack_keys(results[4], H), unstack_keys(results[5], H))
```

```python
from functools import partial

import jax
import jax.numpy as jnp
from jax import lax
from jax.experimental import pallas as pl
from jax.experimental.pallas import tpu as pltpu
from jax.sharding import PartitionSpec as P

HD = 128
BLOCK = 128
LOG2E = 1.4426950408889634
HIDDEN = -1e30
MESH = pl.DeviceIdType.MESH
F32 = jnp.float32
BF16 = jnp.bfloat16


def dot_nt(a, b):
    return lax.dot_general(a, b, (((1,), (1,)), ((), ())), preferred_element_type=F32)


def dot_nn(a, b):
    return jnp.dot(a, b, preferred_element_type=F32)


def fold_max(x):
    return jnp.max(x.reshape(x.shape[0] // 8, 8, x.shape[1]), axis=0)


def fold_sum(x):
    return jnp.sum(x.reshape(x.shape[0] // 8, 8, x.shape[1]), axis=0)


def turned(x):
    return jnp.transpose(x.astype(F32)).astype(BF16)


def kernel(
    ring,
    mask_ref, qc, kc, vc, doc, qh, kh, vh, doh,
    dqc_o, dkc_o, dvc_o, dqh_o, dkh_o, dvh_o,
    kvc, kvh, qdo, ktc, kth, kts, bias_s, e_c, dp_c, e_h, dp_h, st, st_f, st_d,
    acc_h, acc_c, dqp, dq_own, dq_r, xh_r, xc_r, yh_s, yh_r, yc_s, yc_r, zh_s, zh_r,
    a_s, a_r, q_s, q_r, t_s, t_r, d_s, d_r, z_s, z_r, i_s, i_r,
):
    cells = qc.shape[0]
    rows = qh.shape[0]
    heads = qc.shape[1] // HD
    wide = heads * HD
    scale = HD ** (-0.5)
    factor = scale * LOG2E
    me = lax.axis_index("seq")
    hx = lax.axis_index("head")
    core = me % 2
    pos_z = (me // 2) % ring
    pos_y = me // (2 * ring)

    def peer(a, d, b):
        y = (pos_y + a) % 2
        z = (pos_z + d + ring) % ring
        c = (core + b) % 2
        return ((y * ring + z) * 2 + c, hx)

    def rcopy(src, dst, send, recv, to):
        return pltpu.make_async_remote_copy(
            src_ref=src, dst_ref=dst, send_sem=send, recv_sem=recv,
            device_id=to, device_id_type=MESH,
        )

    barrier = pltpu.get_barrier_semaphore()
    for d in range(1, ring):
        pl.semaphore_signal(barrier, inc=1, device_id=peer(0, d, 0), device_id_type=MESH)
    pl.semaphore_signal(barrier, inc=1, device_id=peer(1, 0, 0), device_id_type=MESH)
    pl.semaphore_signal(barrier, inc=1, device_id=peer(0, 0, 1), device_id_type=MESH)

    kvh[0, 0:rows, 0:HD] = kh[...]
    kvh[0, 0:rows, HD : 2 * HD] = vh[...]
    kvc[0, :, 0:HD] = kc[...]
    kvc[0, :, HD : 2 * HD] = vc[...]
    qdo[0:rows, 0:wide] = qh[...]
    qdo[0:rows, wide : 2 * wide] = doh[...]

    pl.semaphore_wait(barrier, ring + 1)

    order = []
    for d in range(1, ring // 2 + 1):
        order.append(d)
        if ring - d != d:
            order.append(ring - d)

    a_cp = {}
    for d in order:
        a_cp[d] = rcopy(
            kvh.at[0, pl.ds(0, rows)], kvh.at[0, pl.ds(d * rows, rows)],
            a_s.at[d], a_r.at[d], peer(0, d, 0),
        )
        a_cp[d].start()
    c_y = rcopy(kvc.at[0], kvc.at[2], i_s.at[0], i_r.at[0], peer(1, 0, 0))
    c_y.start()
    c_c = rcopy(kvc.at[0], kvc.at[1], i_s.at[1], i_r.at[1], peer(0, 0, 1))
    c_c.start()
    q_cp = {}
    for d in order:
        q_cp[d] = rcopy(
            qdo.at[pl.ds(0, rows)], qdo.at[pl.ds(d * rows, rows)],
            q_s.at[d], q_r.at[d], peer(0, d, 0),
        )
        q_cp[d].start()

    lane = lax.broadcasted_iota(jnp.int32, (1, cells), 1)
    for a in range(2):
        for d in range(ring):
            y = (pos_y + a) % 2
            z = (pos_z - d + ring) % ring
            block = (y * ring + z) * 2 * rows // BLOCK
            low = jnp.where(mask_ref[0, block] > 0, 0.0, HIDDEN)
            high = jnp.where(mask_ref[1, block] > 0, 0.0, HIDDEN)
            bias_s[a * ring + d : a * ring + d + 1, :] = jnp.where(lane < BLOCK, low, high)
    acc_h[...] = jnp.zeros_like(acc_h)
    acc_c[...] = jnp.zeros_like(acc_c)
    ktc[0] = turned(kvc[0, :, 0:HD])

    for d in order:
        a_cp[d].wait_recv()
    h_y = rcopy(kvh.at[0], kvh.at[2], i_s.at[3], i_r.at[3], peer(1, 0, 0))
    h_y.start()
    h_c = rcopy(kvh.at[0], kvh.at[1], i_s.at[4], i_r.at[4], peer(0, 0, 1))
    h_c.start()
    c_y.wait_recv()
    c_f = rcopy(kvc.at[2], kvc.at[3], i_s.at[2], i_r.at[2], peer(0, 0, 1))
    c_f.start()
    kth[0] = turned(kvh[0, :, 0:HD])
    h_y.wait_recv()
    h_f = rcopy(kvh.at[2], kvh.at[3], i_s.at[5], i_r.at[5], peer(0, 0, 1))
    h_f.start()
    h_c.wait_recv()
    kth[1] = turned(kvh[1, :, 0:HD])
    kth[2] = turned(kvh[2, :, 0:HD])
    h_f.wait_recv()
    kth[3] = turned(kvh[3, :, 0:HD])

    half = ring * rows // 2
    per = half // rows

    def cell_head(h, carry):
        col = pl.ds(pl.multiple_of(h * HD, HD), HD)
        q = qc[:, col]
        g = doc[:, col]
        top = fold_max(dot_nt(kvc[0, :, 0:HD], q))
        for ab in range(4):
            for p in range(2):
                s = dot_nt(kvh[ab, p * half : (p + 1) * half, 0:HD], q)
                for j in range(per):
                    at = (ab // 2) * ring + p * per + j
                    top = jnp.maximum(
                        top, fold_max(s[j * rows : (j + 1) * rows]) + bias_s[at : at + 1, :]
                    )
        m2 = jnp.max(top, axis=0, keepdims=True) * factor
        s = dot_nt(kvc[0, :, 0:HD], q)
        dp = dot_nt(kvc[0, :, HD : 2 * HD], g)
        e = jnp.exp2(s * factor - m2)
        total = fold_sum(e)
        inner = fold_sum(e * dp)
        e_c[0:cells, :] = e
        dp_c[0:cells, :] = dp
        for ab in range(4):
            for p in range(2):
                s = dot_nt(kvh[ab, p * half : (p + 1) * half, 0:HD], q)
                dp = dot_nt(kvh[ab, p * half : (p + 1) * half, HD : 2 * HD], g)
                base = cells + (2 * ab + p) * half
                dp_c[base : base + half, :] = dp
                for j in range(per):
                    at = (ab // 2) * ring + p * per + j
                    part = slice(j * rows, (j + 1) * rows)
                    e = jnp.exp2(s[part] * factor - (m2 - bias_s[at : at + 1, :]))
                    total = total + fold_sum(e)
                    inner = inner + fold_sum(e * dp[part])
                    e_c[base + j * rows : base + (j + 1) * rows, :] = e
        inv = 1.0 / jnp.sum(total, axis=0, keepdims=True)
        delta = jnp.sum(inner, axis=0, keepdims=True) * inv
        w = e_c[0:cells, :] * inv
        ds = (w * (dp_c[0:cells, :] - delta)).astype(BF16)
        acc_c[0, 0:cells, 0:HD] += dot_nn(ds, q)
        acc_c[0, 0:cells, HD : 2 * HD] += dot_nn(w.astype(BF16), g)
        dq = dot_nn(ktc[0], ds)
        size = 2 * half
        for ab in range(4):
            base = cells + ab * size
            w = e_c[base : base + size, :] * inv
            ds = (w * (dp_c[base : base + size, :] - delta)).astype(BF16)
            acc_h[ab, :, 0:HD] += dot_nn(ds, q)
            acc_h[ab, :, HD : 2 * HD] += dot_nn(w.astype(BF16), g)
            dq = dq + dot_nn(kth[ab], ds)
        dqc_o[:, col] = (jnp.transpose(dq) * scale).astype(BF16)
        return carry

    lax.fori_loop(0, heads, cell_head, 0)

    hx_cp = []
    for a in range(2):
        cp = rcopy(acc_h.at[2 * a + 1], xh_r.at[a], i_s.at[6 + a], i_r.at[6 + a], peer(0, 0, 1))
        cp.start()
        hx_cp.append(cp)

    c_c.wait_recv()
    c_f.wait_recv()
    for ab in range(1, 4):
        ktc[ab] = turned(kvc[ab, :, 0:HD])
    for ab in range(4):
        kts[:, ab * rows : (ab + 1) * rows] = kth[ab, :, 0:rows]
    for d in order:
        q_cp[d].wait_recv()

    lines = ring * rows

    def head_stats(h, carry):
        col = pl.ds(pl.multiple_of(h * HD, HD), HD)
        col_g = pl.ds(pl.multiple_of(wide + h * HD, HD), HD)
        q = qdo[:, col]
        g = qdo[:, col_g]
        top = fold_max(dot_nt(kvc[0, :, 0:HD], q))
        for ab in range(1, 4):
            top = jnp.maximum(top, fold_max(dot_nt(kvc[ab, :, 0:HD], q)))
        for ab in range(4):
            top = jnp.maximum(top, fold_max(dot_nt(kvh[ab, 0:rows, 0:HD], q)))
        m2 = jnp.max(top, axis=0, keepdims=True) * factor
        total = jnp.zeros((8, lines), F32)
        inner = jnp.zeros((8, lines), F32)
        for ab in range(4):
            dp = dot_nt(kvc[ab, :, HD : 2 * HD], g)
            e = jnp.exp2(dot_nt(kvc[ab, :, 0:HD], q) * factor - m2)
            total = total + fold_sum(e)
            inner = inner + fold_sum(e * dp)
            e_h[h, ab * cells : (ab + 1) * cells, :] = e
            dp_h[h, ab * cells : (ab + 1) * cells, :] = dp
        for ab in range(4):
            base = 4 * cells + ab * rows
            dp = dot_nt(kvh[ab, 0:rows, HD : 2 * HD], g)
            e = jnp.exp2(dot_nt(kvh[ab, 0:rows, 0:HD], q) * factor - m2)
            total = total + fold_sum(e)
            inner = inner + fold_sum(e * dp)
            e_h[h, base : base + rows, :] = e
            dp_h[h, base : base + rows, :] = dp
        st[0, 0, pl.ds(h, 1), :] = m2
        st[0, 1, pl.ds(h, 1), :] = jnp.sum(total, axis=0, keepdims=True)
        st[0, 2, pl.ds(h, 1), :] = jnp.sum(inner, axis=0, keepdims=True)
        return carry

    lax.fori_loop(0, heads, head_stats, 0)

    t_cp = {}
    for d in order:
        t_cp[d] = rcopy(st.at[0], st.at[d], t_s.at[d], t_r.at[d], peer(0, d, 0))
        t_cp[d].start()

    for cp in hx_cp:
        cp.wait_recv()
    yh_s[...] = (acc_h[2] + xh_r[1]).astype(BF16)
    hy_cp = rcopy(yh_s, yh_r, i_s.at[8], i_r.at[8], peer(1, 0, 0))
    hy_cp.start()

    for d in order:
        t_cp[d].wait_recv()
    seen = [[st[0, k] for k in range(3)]]
    for d in range(1, ring):
        seen.append([pltpu.roll(st[d, k], d * rows, 1) for k in range(3)])
    best = seen[0][0]
    for d in range(1, ring):
        best = jnp.maximum(best, seen[d][0])
    total = jnp.zeros_like(best)
    inner = jnp.zeros_like(best)
    for d in range(ring):
        lift = jnp.exp2(seen[d][0] - best)
        total = total + seen[d][1] * lift
        inner = inner + seen[d][2] * lift
    inv = 1.0 / total
    st_f[...] = jnp.exp2(st[0, 0] - best) * inv
    st_d[...] = inner * inv

    hy_cp.wait_recv()
    own_h = acc_h[0] + xh_r[0] + yh_r[...].astype(F32)
    acc_h[0] = own_h
    zh_s[...] = own_h.astype(BF16)
    z_cp = {}
    for d in order:
        z_cp[d] = rcopy(
            zh_s.at[pl.ds(d * rows, rows)], zh_r.at[d], z_s.at[d], z_r.at[d], peer(0, -d, 0)
        )
        z_cp[d].start()

    def head_grads(h, carry):
        col = pl.ds(pl.multiple_of(h * HD, HD), HD)
        col_g = pl.ds(pl.multiple_of(wide + h * HD, HD), HD)
        q = qdo[:, col]
        g = qdo[:, col_g]
        f = st_f[pl.ds(h, 1), :]
        delta = st_d[pl.ds(h, 1), :]
        dq = jnp.zeros((HD, lines), F32)
        for ab in range(4):
            part = slice(ab * cells, (ab + 1) * cells)
            w = e_h[h, part, :] * f
            ds = (w * (dp_h[h, part, :] - delta)).astype(BF16)
            acc_c[ab, 0:cells, 0:HD] += dot_nn(ds, q)
            acc_c[ab, 0:cells, HD : 2 * HD] += dot_nn(w.astype(BF16), g)
            dq = dq + dot_nn(ktc[ab], ds)
        part = slice(4 * cells, 4 * cells + 4 * rows)
        w = e_h[h, part, :] * f
        ds = (w * (dp_h[h, part, :] - delta)).astype(BF16)
        dk = dot_nn(ds, q)
        dv = dot_nn(w.astype(BF16), g)
        for ab in range(4):
            acc_c[ab, cells : cells + rows, 0:HD] += dk[ab * rows : (ab + 1) * rows]
            acc_c[ab, cells : cells + rows, HD : 2 * HD] += dv[ab * rows : (ab + 1) * rows]
        dq = dq + dot_nn(kts[...], ds)
        flat = jnp.transpose(dq) * scale
        dq_own[:, col] = flat[0:rows]
        dqp[:, col] = flat.astype(BF16)
        for d in order:
            rcopy(
                dqp.at[pl.ds(d * rows, rows), col], dq_r.at[d, :, col],
                d_s.at[d], d_r.at[d], peer(0, -d, 0),
            ).start()
        return carry

    lax.fori_loop(0, heads, head_grads, 0)

    cx_cp = []
    for a in (1, 0):
        cp = rcopy(acc_c.at[2 * a + 1], xc_r.at[a], i_s.at[9 + a], i_r.at[9 + a], peer(0, 0, 1))
        cp.start()
        cx_cp.append(cp)
    cx_cp[0].wait_recv()
    yc_s[...] = (acc_c[2] + xc_r[1]).astype(BF16)
    cy_cp = rcopy(yc_s, yc_r, i_s.at[11], i_r.at[11], peer(1, 0, 0))
    cy_cp.start()

    for d in order:
        z_cp[d].wait_recv()
    own_h = acc_h[0, 0:rows]
    for d in range(1, ring):
        own_h = own_h + zh_r[d].astype(F32)
    cx_cp[1].wait_recv()
    own_c = acc_c[0] + xc_r[0]

    d_cp = {}
    for d in order:
        d_cp[d] = rcopy(
            dqp.at[pl.ds(d * rows, rows)], dq_r.at[d], d_s.at[d], d_r.at[d], peer(0, -d, 0)
        )
        d_cp[d].wait_recv()
    dq = dq_own[...]
    for d in range(1, ring):
        dq = dq + dq_r[d].astype(F32)
    dqh_o[...] = dq.astype(BF16)

    cy_cp.wait_recv()
    own_c = own_c + yc_r[...].astype(F32)
    dkc_o[...] = (own_c[0:cells, 0:HD] * scale).astype(BF16)
    dvc_o[...] = own_c[0:cells, HD : 2 * HD].astype(BF16)
    own_h = own_h + own_c[cells : cells + rows]
    dkh_o[...] = (own_h[:, 0:HD] * scale).astype(BF16)
    dvh_o[...] = own_h[:, HD : 2 * HD].astype(BF16)

    for group in (a_cp, q_cp, t_cp, z_cp, d_cp):
        for d in order:
            group[d].wait_send()
    for cp in [c_y, c_c, c_f, h_y, h_c, h_f, hy_cp, cy_cp] + hx_cp + cx_cp:
        cp.wait_send()


def per_device(ring, q_cells, k_cells, v_cells, do_cells, q_head, k_head, v_head, do_head, vis_mask):
    cells = q_cells.shape[0]
    rows = q_head.shape[0]
    wide = q_cells.shape[1]
    heads = wide // HD
    lines = ring * rows
    keys_c = cells + 4 * lines
    keys_h = 4 * cells + 4 * rows
    ext = cells + rows
    vmem = pl.BlockSpec(memory_space=pltpu.VMEM)
    dma = pltpu.SemaphoreType.DMA
    return pl.pallas_call(
        partial(kernel, ring),
        out_shape=[
            jax.ShapeDtypeStruct((cells, wide), BF16),
            jax.ShapeDtypeStruct((cells, HD), BF16),
            jax.ShapeDtypeStruct((cells, HD), BF16),
            jax.ShapeDtypeStruct((rows, wide), BF16),
            jax.ShapeDtypeStruct((rows, HD), BF16),
            jax.ShapeDtypeStruct((rows, HD), BF16),
        ],
        in_specs=[pl.BlockSpec(memory_space=pltpu.SMEM)] + [vmem] * 8,
        out_specs=[vmem] * 6,
        scratch_shapes=[
            pltpu.VMEM((4, cells, 2 * HD), BF16),
            pltpu.VMEM((4, lines, 2 * HD), BF16),
            pltpu.VMEM((lines, 2 * wide), BF16),
            pltpu.VMEM((4, HD, cells), BF16),
            pltpu.VMEM((4, HD, lines), BF16),
            pltpu.VMEM((HD, 4 * rows), BF16),
            pltpu.VMEM((2 * ring, cells), F32),
            pltpu.VMEM((keys_c, cells), F32),
            pltpu.VMEM((keys_c, cells), F32),
            pltpu.VMEM((heads, keys_h, lines), F32),
            pltpu.VMEM((heads, keys_h, lines), F32),
            pltpu.VMEM((ring, 3, heads, lines), F32),
            pltpu.VMEM((heads, lines), F32),
            pltpu.VMEM((heads, lines), F32),
            pltpu.VMEM((4, lines, 2 * HD), F32),
            pltpu.VMEM((4, ext, 2 * HD), F32),
            pltpu.VMEM((lines, wide), BF16),
            pltpu.VMEM((rows, wide), F32),
            pltpu.VMEM((ring, rows, wide), BF16),
            pltpu.VMEM((2, lines, 2 * HD), F32),
            pltpu.VMEM((2, ext, 2 * HD), F32),
            pltpu.VMEM((lines, 2 * HD), BF16),
            pltpu.VMEM((lines, 2 * HD), BF16),
            pltpu.VMEM((ext, 2 * HD), BF16),
            pltpu.VMEM((ext, 2 * HD), BF16),
            pltpu.VMEM((lines, 2 * HD), BF16),
            pltpu.VMEM((ring, rows, 2 * HD), BF16),
        ]
        + [dma((ring,))] * 10
        + [dma((12,))] * 2,
        compiler_params=pltpu.CompilerParams(
            collective_id=0, has_side_effects=True, vmem_limit_bytes=60 * 1024 * 1024
        ),
    )(vis_mask, q_cells, k_cells, v_cells, do_cells, q_head, k_head, v_head, do_head)


def solution(mesh):
    both = P("seq", "head")
    return jax.shard_map(
        partial(per_device, mesh.shape["seq"] // 4),
        mesh=mesh,
        in_specs=(both,) * 8 + (P("seq", None),),
        out_specs=(both,) * 6,
        check_vma=False,
    )
```

```python
from functools import partial

import jax
import jax.numpy as jnp
from jax import lax
from jax.experimental import pallas as pl
from jax.experimental.pallas import tpu as pltpu
from jax.sharding import PartitionSpec as P

HD = 128
BLOCK = 128
LOG2E = 1.4426950408889634
HIDDEN = -1e30
MESH = pl.DeviceIdType.MESH
F32 = jnp.float32
BF16 = jnp.bfloat16


def dot_nt(a, b):
    return lax.dot_general(a, b, (((1,), (1,)), ((), ())), preferred_element_type=F32)


def dot_nn(a, b):
    return jnp.dot(a, b, preferred_element_type=F32)


def fold_max(x):
    return jnp.max(x.reshape(x.shape[0] // 8, 8, x.shape[1]), axis=0)


def fold_sum(x):
    return jnp.sum(x.reshape(x.shape[0] // 8, 8, x.shape[1]), axis=0)


def turned(x):
    return jnp.transpose(x.astype(F32)).astype(BF16)


def kernel(
    ring,
    mask_ref, qc_i, kc_i, vc_i, doc_i, qh_i, kh_i, vh_i, doh_i,
    dqc_o, dkc_o, dvc_o, dqh_o, dkh_o, dvh_o,
    qc, doc, dqc, in_s, kvc, kvh, qdo, ktc, kth, bias_s, e_c, dp_c, s_c, e_h, dp_h, m_h, st, st_f, st_d,
    acc_h, acc_c, dqp, dq_own, dq_r, dq_x, dq_m, xh_r, xc_r, yh_s, yh_r, yc_s, yc_r, zh_s, zh_r,
    a_s, a_r, q_s, q_r, t_s, t_r, d_s, d_r, z_s, z_r, i_s, i_r,
):
    cells = qc.shape[0]
    rows = qh_i.shape[0]
    heads = qc.shape[1] // HD
    half = heads // 2
    wide = heads * HD
    ext = cells + rows
    lines = ring * rows
    scale = HD ** (-0.5)
    factor = scale * LOG2E
    me = lax.axis_index("seq")
    hx = lax.axis_index("head")
    core = me % 2
    pos_z = (me // 2) % ring
    pos_y = me // (2 * ring)

    def peer(a, d, b):
        y = (pos_y + a) % 2
        z = (pos_z + d + ring) % ring
        c = (core + b) % 2
        return ((y * ring + z) * 2 + c, hx)

    def rcopy(src, dst, send, recv, to):
        return pltpu.make_async_remote_copy(
            src_ref=src, dst_ref=dst, send_sem=send, recv_sem=recv,
            device_id=to, device_id_type=MESH,
        )

    barrier = pltpu.get_barrier_semaphore()
    for d in range(1, ring):
        pl.semaphore_signal(barrier, inc=1, device_id=peer(0, d, 0), device_id_type=MESH)
    pl.semaphore_signal(barrier, inc=1, device_id=peer(1, 0, 0), device_id_type=MESH)
    pl.semaphore_signal(barrier, inc=1, device_id=peer(0, 0, 1), device_id_type=MESH)

    side = half * HD
    moves = [
        (kh_i, kvh.at[0, pl.ds(0, rows), pl.ds(0, HD)]),
        (vh_i, kvh.at[0, pl.ds(0, rows), pl.ds(HD, HD)]),
        (kc_i, kvc.at[0, pl.ds(0, cells), pl.ds(0, HD)]),
        (vc_i, kvc.at[0, pl.ds(0, cells), pl.ds(HD, HD)]),
        (kh_i, kvc.at[0, pl.ds(cells, rows), pl.ds(0, HD)]),
        (vh_i, kvc.at[0, pl.ds(cells, rows), pl.ds(HD, HD)]),
    ]
    for p in range(2):
        part = pl.ds(p * side, side)
        moves.append((qh_i.at[:, part], qdo.at[pl.ds(0, rows), pl.ds(p * wide, side)]))
        moves.append((doh_i.at[:, part], qdo.at[pl.ds(0, rows), pl.ds(p * wide + side, side)]))
    moves += [(qc_i, qc), (doc_i, doc)]
    moves = [pltpu.make_async_copy(x, y, in_s.at[n]) for n, (x, y) in enumerate(moves)]
    for cp in moves:
        cp.start()
    for cp in moves[:-2]:
        cp.wait()

    pl.semaphore_wait(barrier, ring + 1)

    order = []
    for d in range(1, ring // 2 + 1):
        order.append(d)
        if ring - d != d:
            order.append(ring - d)

    far = ring // 2
    cut = rows // 2

    def q_send(slot, step, p):
        to = (slot + step) % ring
        low, size, sem = slot * rows, rows, to
        if to == far:
            size = cut
            if step == -1:
                low, sem = low + cut, 0
        shift = step * rows if slot or step == 1 else (ring - 1) * rows
        lanes = pl.ds(p * wide, wide)
        return rcopy(
            qdo.at[pl.ds(low, size), lanes], qdo.at[pl.ds(low + shift, size), lanes],
            q_s.at[p * ring + sem], q_r.at[p * ring + sem], peer(0, step, 0),
        )

    def q_step(k, p):
        for slot, step in ((k, 1), ((ring - k) % ring, -1)):
            if k:
                q_send((slot - step) % ring, step, p).wait_recv()
            q_send(slot, step, p).start()

    def q_last(p):
        q_send(far - 1, 1, p).wait_recv()
        q_send(far + 1, -1, p).wait_recv()

    a_cp = {}
    for d in order:
        a_cp[d] = rcopy(
            kvh.at[0, pl.ds(0, rows)], kvh.at[0, pl.ds(d * rows, rows)],
            a_s.at[d], a_r.at[d], peer(0, d, 0),
        )
        a_cp[d].start()
    c_y = rcopy(kvc.at[0], kvc.at[2], i_s.at[0], i_r.at[0], peer(1, 0, 0))
    c_y.start()
    c_c = rcopy(kvc.at[0], kvc.at[1], i_s.at[1], i_r.at[1], peer(0, 0, 1))
    c_c.start()
    q_step(0, 0)
    q_step(0, 1)

    lane = lax.broadcasted_iota(jnp.int32, (1, cells), 1)
    for a in range(2):
        for d in range(ring):
            y = (pos_y + a) % 2
            z = (pos_z - d + ring) % ring
            block = (y * ring + z) * 2 * rows // BLOCK
            low = jnp.where(mask_ref[0, block] > 0, 0.0, HIDDEN)
            high = jnp.where(mask_ref[1, block] > 0, 0.0, HIDDEN)
            row = jnp.where(lane < BLOCK, low, high)
            bias_s[a, d * rows : (d + 1) * rows, :] = jnp.broadcast_to(row, (rows, cells))
    acc_h[...] = jnp.zeros_like(acc_h)
    acc_c[...] = jnp.zeros_like(acc_c)

    def column(h):
        return pl.ds(pl.multiple_of(h * HD, HD), HD)

    def cell_local(h, carry):
        q, g = qc[:, column(h)], doc[:, column(h)]
        s = dot_nt(kvc[0, 0:cells, 0:HD], q)
        dp = dot_nt(kvc[0, 0:cells, HD : 2 * HD], g)
        m2 = jnp.max(fold_max(s), axis=0, keepdims=True) * factor
        e = jnp.exp2(s * factor - m2)
        e_c[h, 0:cells, :] = e
        dp_c[h, 0:cells, :] = dp
        s_c[h, 0:1, :] = m2
        s_c[h, 8:9, :] = jnp.sum(fold_sum(e), axis=0, keepdims=True)
        s_c[h, 16:17, :] = jnp.sum(fold_sum(e * dp), axis=0, keepdims=True)
        return carry

    def cell_block(ab, h, carry):
        q, g = qc[:, column(h)], doc[:, column(h)]
        base = cells + ab * lines
        s = dot_nt(kvh[ab, :, 0:HD], q)
        dp = dot_nt(kvh[ab, :, HD : 2 * HD], g)
        s = s * factor + bias_s[ab // 2]
        m2 = jnp.max(fold_max(s), axis=0, keepdims=True)
        e = jnp.exp2(s - m2)
        e_c[h, base : base + lines, :] = e
        dp_c[h, base : base + lines, :] = dp
        s_c[h, ab + 1 : ab + 2, :] = m2
        s_c[h, ab + 9 : ab + 10, :] = jnp.sum(fold_sum(e), axis=0, keepdims=True)
        s_c[h, ab + 17 : ab + 18, :] = jnp.sum(fold_sum(e * dp), axis=0, keepdims=True)
        return carry

    def cell_blocks(ab, hooks):
        def body(h, carry):
            for at, step in hooks:

                @pl.when(h == at)
                def _():
                    q_step(*step)

            return cell_block(ab, h, carry)

        lax.fori_loop(0, heads, body, 0)

    for cp in moves[-2:]:
        cp.wait()
    lax.fori_loop(0, heads, cell_local, 0)
    ktc[0] = turned(kvc[0, :, 0:HD])
    for d in order:
        a_cp[d].wait_recv()
    h_y = rcopy(kvh.at[0], kvh.at[2], i_s.at[3], i_r.at[3], peer(1, 0, 0))
    h_y.start()
    h_c = rcopy(kvh.at[0], kvh.at[1], i_s.at[4], i_r.at[4], peer(0, 0, 1))
    h_c.start()
    c_y.wait_recv()
    c_f = rcopy(kvc.at[2], kvc.at[3], i_s.at[2], i_r.at[2], peer(0, 0, 1))
    c_f.start()
    cell_blocks(0, ())
    h_c.wait_recv()
    cell_blocks(1, ((2, (1, 0)), (7, (1, 1))))
    kth[0] = turned(kvh[0, :, 0:HD])
    kth[1] = turned(kvh[1, :, 0:HD])
    c_c.wait_recv()
    ktc[1] = turned(kvc[1, :, 0:HD])
    ktc[2] = turned(kvc[2, :, 0:HD])
    c_f.wait_recv()
    ktc[3] = turned(kvc[3, :, 0:HD])
    h_y.wait_recv()
    h_f = rcopy(kvh.at[2], kvh.at[3], i_s.at[5], i_r.at[5], peer(0, 0, 1))
    h_f.start()
    kth[2] = turned(kvh[2, :, 0:HD])
    cell_blocks(2, ((4, (2, 0)),))
    h_f.wait_recv()
    cell_blocks(3, ((2, (2, 1)),))
    kth[3] = turned(kvh[3, :, 0:HD])

    def cell_grads(h, carry):
        for at, step in ((2, (3, 0)), (4, (3, 1))):

            @pl.when(h == at)
            def _():
                q_step(*step)

        q, g = qc[:, column(h)], doc[:, column(h)]
        tops = s_c[h, 0:5, :]
        best = jnp.max(tops, axis=0, keepdims=True)
        lift = jnp.exp2(tops - best)
        total = jnp.sum(s_c[h, 8:13, :] * lift, axis=0, keepdims=True)
        inner = jnp.sum(s_c[h, 16:21, :] * lift, axis=0, keepdims=True)
        inv = 1.0 / total
        delta = inner * inv
        lift = lift * inv
        w = e_c[h, 0:cells, :] * lift[0:1]
        ds = (w * (dp_c[h, 0:cells, :] - delta)).astype(BF16)
        acc_c[0, 0:cells, 0:HD] += dot_nn(ds, q)
        acc_c[0, 0:cells, HD : 2 * HD] += dot_nn(w.astype(BF16), g)
        dq = dot_nn(ktc[0, :, 0:cells], ds)
        for ab in range(4):
            part = slice(cells + ab * lines, cells + (ab + 1) * lines)
            w = e_c[h, part, :] * lift[ab + 1 : ab + 2]
            ds = (w * (dp_c[h, part, :] - delta)).astype(BF16)
            acc_h[ab, :, 0:HD] += dot_nn(ds, q)
            acc_h[ab, :, HD : 2 * HD] += dot_nn(w.astype(BF16), g)
            dq = dq + dot_nn(kth[ab], ds)
        dqc[:, column(h)] = (jnp.transpose(dq) * scale).astype(BF16)
        return carry

    lax.fori_loop(0, heads, cell_grads, 0)

    dqc_cp = pltpu.make_async_copy(dqc, dqc_o, in_s.at[12])
    dqc_cp.start()
    hx_cp = []
    for a in (1, 0):
        cp = rcopy(acc_h.at[2 * a + 1], xh_r.at[a], i_s.at[6 + a], i_r.at[6 + a], peer(0, 0, 1))
        cp.start()
        hx_cp.append(cp)

    hy_cp = rcopy(yh_s, yh_r, i_s.at[8], i_r.at[8], peer(1, 0, 0))

    def grouped(p, h):
        return (
            qdo[:, pl.ds(pl.multiple_of((p * heads + h) * HD, HD), HD)],
            qdo[:, pl.ds(pl.multiple_of((p * heads + half + h) * HD, HD), HD)],
        )

    def head_stats(p, h, carry):
        q, g = grouped(p, h)
        tops, totals, inners = [], [], []
        for ab in range(4):
            s = dot_nt(kvc[ab, :, 0:HD], q)
            dp = dot_nt(kvc[ab, :, HD : 2 * HD], g)
            m2 = jnp.max(fold_max(s), axis=0, keepdims=True) * factor
            e = jnp.exp2(s * factor - m2)
            e_h[p * half + h, ab * ext : (ab + 1) * ext, :] = e
            dp_h[p * half + h, ab * ext : (ab + 1) * ext, :] = dp
            m_h[p * half + h, ab : ab + 1, :] = m2
            tops.append(m2)
            totals.append(jnp.sum(fold_sum(e), axis=0, keepdims=True))
            inners.append(jnp.sum(fold_sum(e * dp), axis=0, keepdims=True))
        best = jnp.maximum(jnp.maximum(tops[0], tops[1]), jnp.maximum(tops[2], tops[3]))
        total = jnp.zeros_like(best)
        inner = jnp.zeros_like(best)
        for ab in range(4):
            lift = jnp.exp2(tops[ab] - best)
            total = total + totals[ab] * lift
            inner = inner + inners[ab] * lift
        st[p, 0, pl.ds(h, 1), :] = best + jnp.log(total) * LOG2E
        st[p, 0, pl.ds(half + h, 1), :] = inner / total
        return carry

    t_cp = {}
    for p in range(2):
        q_last(p)

        def body(h, carry):
            if p == 0:

                @pl.when(h == half - 1)
                def _():
                    hx_cp[0].wait_recv()
                    yh_s[...] = (acc_h[2] + xh_r[1]).astype(BF16)
                    hy_cp.start()

            return head_stats(p, h, carry)

        lax.fori_loop(0, half, body, 0)
        for d in order:
            t_cp[p, d] = rcopy(
                st.at[p, 0], st.at[p, d], t_s.at[p * ring + d], t_r.at[p * ring + d],
                peer(0, d, 0),
            )
            t_cp[p, d].start()

    def merge(p):
        for d in order:
            t_cp[p, d].wait_recv()
        seen = [st[p, 0]]
        for d in range(1, ring):
            seen.append(pltpu.roll(st[p, d], d * rows, 1))
        best = seen[0][0:half]
        for d in range(1, ring):
            best = jnp.maximum(best, seen[d][0:half])
        total = jnp.zeros_like(best)
        inner = jnp.zeros_like(best)
        for d in range(ring):
            lift = jnp.exp2(seen[d][0:half] - best)
            total = total + lift
            inner = inner + seen[d][half : 2 * half] * lift
        st_f[p, 0:half] = best + jnp.log(total) * LOG2E
        st_d[p, 0:half] = inner / total

    near = 2
    first = (far, 0, near + 1, ring - near - 1, 1, ring - 1)

    def dq_send(key, p, lanes):
        low, size, slot = 0, rows, key
        if key in (1, ring - 1):
            step = -1 if key == 1 else 1
            target = dq_r.at[0 if key == 1 else 1]
        elif key in (near + 1, ring - near - 1):
            step = -1 if key == near + 1 else 1
            target = dq_x.at[0 if key == near + 1 else 1]
        elif key in (far, 0):
            step = -near if key == far else near
            slot, size, low = far, cut, 0 if key == far else cut
            target = dq_x.at[2]
        else:
            step = -near if key == near else near
            target = dq_r.at[2 if key == near else 3]
        if key in (near, ring - near):
            source = dq_m.at[0 if key == near else 1, pl.ds(0, rows), lanes]
        else:
            source = dqp.at[pl.ds(slot * rows + low, size), lanes]
        return rcopy(
            source, target.at[pl.ds(low, size), lanes],
            d_s.at[p * ring + key], d_r.at[p * ring + key], peer(0, step, 0),
        )

    def lanes_of(p):
        return pl.ds(p * side, side)

    def combine(p):
        lanes = lanes_of(p)
        for key in (far, 0, near + 1, ring - near - 1):
            dq_send(key, p, lanes).wait_recv()
        for n in range(2):
            own = dq_own[1 + n, :, lanes] + dq_x[n, :, lanes].astype(F32)
            part = slice(n * cut, (n + 1) * cut)
            rest = slice((1 - n) * cut, (2 - n) * cut)
            dq_m[n, part, lanes] = (own[part] + dq_x[2, part, lanes].astype(F32)).astype(BF16)
            dq_m[n, rest, lanes] = own[rest].astype(BF16)
        for key in (near, ring - near):
            dq_send(key, p, lanes).start()

    def head_grads(p, h, carry):
        q, g = grouped(p, h)
        at = p * half + h
        lift = jnp.exp2(m_h[at, 0:4, :] - st_f[p, pl.ds(h, 1), :])
        delta = st_d[p, pl.ds(h, 1), :]
        dq = jnp.zeros((HD, lines), F32)
        for ab in range(4):
            part = slice(ab * ext, (ab + 1) * ext)
            w = e_h[at, part, :] * lift[ab : ab + 1]
            ds = (w * (dp_h[at, part, :] - delta)).astype(BF16)
            acc_c[ab, :, 0:HD] += dot_nn(ds, q)
            acc_c[ab, :, HD : 2 * HD] += dot_nn(w.astype(BF16), g)
            dq = dq + dot_nn(ktc[ab], ds)
        flat = jnp.transpose(dq) * scale
        for n, slot in enumerate((0, near, ring - near)):
            dq_own[n, :, column(at)] = flat[slot * rows : (slot + 1) * rows]
        dqp[:, column(at)] = flat.astype(BF16)
        for key in first:
            dq_send(key, p, column(at)).start()
        return carry

    hx_cp[1].wait_recv()
    own_h = acc_h[0] + xh_r[0]
    hy_cp.wait_recv()
    own_h = own_h + yh_r[...].astype(F32)
    acc_h[0, 0:rows] = own_h[0:rows]
    zh_s[...] = own_h.astype(BF16)
    z_cp = {}
    for d in order:
        z_cp[d] = rcopy(
            zh_s.at[pl.ds(d * rows, rows)], zh_r.at[d], z_s.at[d], z_r.at[d], peer(0, -d, 0)
        )
        z_cp[d].start()

    merge(0)
    lax.fori_loop(0, half, partial(head_grads, 0), 0)
    merge(1)
    lax.fori_loop(0, half, partial(head_grads, 1), 0)

    cx_cp = []
    for a in (1, 0):
        cp = rcopy(acc_c.at[2 * a + 1], xc_r.at[a], i_s.at[9 + a], i_r.at[9 + a], peer(0, 0, 1))
        cp.start()
        cx_cp.append(cp)
    combine(0)
    cx_cp[0].wait_recv()
    yc_s[...] = (acc_c[2] + xc_r[1]).astype(BF16)
    cy_cp = rcopy(yc_s, yc_r, i_s.at[11], i_r.at[11], peer(1, 0, 0))
    cy_cp.start()

    combine(1)
    cx_cp[1].wait_recv()
    acc_c[0] = acc_c[0] + xc_r[0]

    d_cp = {}
    for p in range(2):
        for key in range(ring):
            d_cp[p, key] = dq_send(key, p, lanes_of(p))
        for key in (1, ring - 1, near, ring - near):
            d_cp[p, key].wait_recv()
    dq = dq_own[0]
    for n in range(4):
        dq = dq + dq_r[n].astype(F32)
    dqh_o[...] = dq.astype(BF16)

    for d in order:
        z_cp[d].wait_recv()
    own_h = acc_h[0, 0:rows]
    for d in range(1, ring):
        own_h = own_h + zh_r[d].astype(F32)
    cy_cp.wait_recv()
    own_c = acc_c[0] + yc_r[...].astype(F32)
    dkc_o[...] = (own_c[0:cells, 0:HD] * scale).astype(BF16)
    dvc_o[...] = own_c[0:cells, HD : 2 * HD].astype(BF16)
    own_h = own_h + own_c[cells:ext]
    dkh_o[...] = (own_h[:, 0:HD] * scale).astype(BF16)
    dvh_o[...] = own_h[:, HD : 2 * HD].astype(BF16)

    dqc_cp.wait()
    for group in (a_cp, z_cp, d_cp, t_cp):
        for cp in group.values():
            cp.wait_send()
    for p in range(2):
        for k in range(far):
            q_send(k, 1, p).wait_send()
            q_send((ring - k) % ring, -1, p).wait_send()
    for cp in [c_y, c_c, c_f, h_y, h_c, h_f, hy_cp, cy_cp] + hx_cp + cx_cp:
        cp.wait_send()


def put_out(*refs):
    count = len(refs) // 2
    sems = refs[-1]
    copies = [
        pltpu.make_async_copy(refs[i], refs[count + i], sems.at[i]) for i in range(count)
    ]
    for cp in copies:
        cp.start()
    for cp in copies:
        cp.wait()


def per_device(ring, q_cells, k_cells, v_cells, do_cells, q_head, k_head, v_head, do_head, vis_mask):
    cells = q_cells.shape[0]
    rows = q_head.shape[0]
    wide = q_cells.shape[1]
    heads = wide // HD
    lines = ring * rows
    half = heads // 2
    ext = cells + rows
    vmem = pl.BlockSpec(memory_space=pltpu.VMEM)
    anywhere = pl.BlockSpec(memory_space=pl.ANY)
    dma = pltpu.SemaphoreType.DMA
    results = pl.pallas_call(
        partial(kernel, ring),
        out_shape=[
            jax.ShapeDtypeStruct((cells, wide), BF16),
            jax.ShapeDtypeStruct((cells, HD), BF16),
            jax.ShapeDtypeStruct((cells, HD), BF16),
            jax.ShapeDtypeStruct((rows, wide), BF16),
            jax.ShapeDtypeStruct((rows, HD), BF16),
            jax.ShapeDtypeStruct((rows, HD), BF16),
        ],
        in_specs=[pl.BlockSpec(memory_space=pltpu.SMEM)] + [anywhere] * 8,
        out_specs=[anywhere] + [vmem] * 5,
        scratch_shapes=[
            pltpu.VMEM((cells, wide), BF16),
            pltpu.VMEM((cells, wide), BF16),
            pltpu.VMEM((cells, wide), BF16),
            dma((13,)),
            pltpu.VMEM((4, ext, 2 * HD), BF16),
            pltpu.VMEM((4, lines, 2 * HD), BF16),
            pltpu.VMEM((lines, 2 * wide), BF16),
            pltpu.VMEM((4, HD, ext), BF16),
            pltpu.VMEM((4, HD, lines), BF16),
            pltpu.VMEM((2, lines, cells), F32),
            pltpu.VMEM((heads, cells + 4 * lines, cells), F32),
            pltpu.VMEM((heads, cells + 4 * lines, cells), F32),
            pltpu.VMEM((heads, 24, cells), F32),
            pltpu.VMEM((heads, 4 * ext, lines), F32),
            pltpu.VMEM((heads, 4 * ext, lines), F32),
            pltpu.VMEM((heads, 8, lines), F32),
            pltpu.VMEM((2, ring, 2 * half, lines), F32),
            pltpu.VMEM((2, 8, lines), F32),
            pltpu.VMEM((2, 8, lines), F32),
            pltpu.VMEM((4, lines, 2 * HD), F32),
            pltpu.VMEM((4, ext, 2 * HD), F32),
            pltpu.VMEM((lines, wide), BF16),
            pltpu.VMEM((3, rows, wide), F32),
            pltpu.VMEM((4, rows, wide), BF16),
            pltpu.VMEM((3, rows, wide), BF16),
            pltpu.VMEM((2, rows, wide), BF16),
            pltpu.VMEM((2, lines, 2 * HD), F32),
            pltpu.VMEM((2, ext, 2 * HD), F32),
            pltpu.VMEM((lines, 2 * HD), BF16),
            pltpu.VMEM((lines, 2 * HD), BF16),
            pltpu.VMEM((ext, 2 * HD), BF16),
            pltpu.VMEM((ext, 2 * HD), BF16),
            pltpu.VMEM((lines, 2 * HD), BF16),
            pltpu.VMEM((ring, rows, 2 * HD), BF16),
        ]
        + [dma((ring,))] * 2
        + [dma((2 * ring,))] * 6
        + [dma((ring,))] * 2
        + [dma((12,))] * 2,
        compiler_params=pltpu.CompilerParams(
            collective_id=0, has_side_effects=True, vmem_limit_bytes=60 * 1024 * 1024
        ),
    )(vis_mask, q_cells, k_cells, v_cells, do_cells, q_head, k_head, v_head, do_head)
    return pl.pallas_call(
        put_out,
        out_shape=[jax.ShapeDtypeStruct(r.shape, r.dtype) for r in results],
        in_specs=[anywhere] * len(results),
        out_specs=[vmem] * len(results),
        scratch_shapes=[dma((len(results),))],
    )(*results)


def solution(mesh):
    both = P("seq", "head")
    return jax.shard_map(
        partial(per_device, mesh.shape["seq"] // 4),
        mesh=mesh,
        in_specs=(both,) * 8 + (P("seq", None),),
        out_specs=(both,) * 6,
        check_vma=False,
    )
```

```python
from functools import partial

import jax
import jax.numpy as jnp
from jax import lax
from jax.experimental import pallas as pl
from jax.experimental.pallas import tpu as pltpu
from jax.sharding import PartitionSpec as P

HD = 128
BLOCK = 128
LOG2E = 1.4426950408889634
HIDDEN = -1e30
MESH = pl.DeviceIdType.MESH
F32 = jnp.float32
BF16 = jnp.bfloat16


def dot_nt(a, b):
    return lax.dot_general(a, b, (((1,), (1,)), ((), ())), preferred_element_type=F32)


def dot_nn(a, b):
    return jnp.dot(a, b, preferred_element_type=F32)


def fold_max(x):
    return jnp.max(x.reshape(x.shape[0] // 8, 8, x.shape[1]), axis=0)


def fold_sum(x):
    return jnp.sum(x.reshape(x.shape[0] // 8, 8, x.shape[1]), axis=0)


def turned(x):
    return jnp.transpose(x.astype(F32)).astype(BF16)


def kernel(
    ring,
    mask_ref, qc_i, kc_i, vc_i, doc_i, qh_i, kh_i, vh_i, doh_i,
    dqc_o, dkc_o, dvc_o, dqh_o, dkh_o, dvh_o,
    qc, doc, dqc, in_s, kvc, kvh, qdo, ktc, kth, bias_s, e_0, e_1, dp_0, dp_1, s_c, e_h, dp_h, m_h, st, st_f, st_d,
    acc_h, acc_c, dqp, dq_own, dq_r, dq_x, dq_m, xh_r, xc_r, yh_s, yh_r, yc_s, yc_r, zh_s, zh_r,
    a_s, a_r, q_s, q_r, t_s, t_r, d_s, d_r, z_s, z_r, i_s, i_r,
):
    cells = qc.shape[0]
    rows = qh_i.shape[0]
    heads = qc.shape[1] // HD
    half = heads // 2
    wide = heads * HD
    ext = cells + rows
    lines = ring * rows
    scale = HD ** (-0.5)
    factor = scale * LOG2E
    me = lax.axis_index("seq")
    hx = lax.axis_index("head")
    core = me % 2
    pos_z = (me // 2) % ring
    pos_y = me // (2 * ring)

    def peer(a, d, b):
        y = (pos_y + a) % 2
        z = (pos_z + d + ring) % ring
        c = (core + b) % 2
        return ((y * ring + z) * 2 + c, hx)

    def rcopy(src, dst, send, recv, to):
        return pltpu.make_async_remote_copy(
            src_ref=src, dst_ref=dst, send_sem=send, recv_sem=recv,
            device_id=to, device_id_type=MESH,
        )

    barrier = pltpu.get_barrier_semaphore()
    for d in range(1, ring):
        pl.semaphore_signal(barrier, inc=1, device_id=peer(0, d, 0), device_id_type=MESH)
    pl.semaphore_signal(barrier, inc=1, device_id=peer(1, 0, 0), device_id_type=MESH)
    pl.semaphore_signal(barrier, inc=1, device_id=peer(0, 0, 1), device_id_type=MESH)

    side = half * HD
    moves = [
        (kh_i, kvh.at[0, pl.ds(0, rows), pl.ds(0, HD)]),
        (vh_i, kvh.at[0, pl.ds(0, rows), pl.ds(HD, HD)]),
        (kc_i, kvc.at[0, pl.ds(0, cells), pl.ds(0, HD)]),
        (vc_i, kvc.at[0, pl.ds(0, cells), pl.ds(HD, HD)]),
        (kh_i, kvc.at[0, pl.ds(cells, rows), pl.ds(0, HD)]),
        (vh_i, kvc.at[0, pl.ds(cells, rows), pl.ds(HD, HD)]),
    ]
    for p in range(2):
        part = pl.ds(p * side, side)
        moves.append((qh_i.at[:, part], qdo.at[pl.ds(0, rows), pl.ds(p * wide, side)]))
        moves.append((doh_i.at[:, part], qdo.at[pl.ds(0, rows), pl.ds(p * wide + side, side)]))
    moves += [(qc_i, qc), (doc_i, doc)]
    moves = [pltpu.make_async_copy(x, y, in_s.at[n]) for n, (x, y) in enumerate(moves)]
    for cp in moves:
        cp.start()
    for cp in moves[:-2]:
        cp.wait()

    pl.semaphore_wait(barrier, ring + 1)

    order = []
    for d in range(1, ring // 2 + 1):
        order.append(d)
        if ring - d != d:
            order.append(ring - d)

    far = ring // 2
    cut = rows // 2

    def q_send(slot, step, p):
        to = (slot + step) % ring
        low, size, sem = slot * rows, rows, to
        if to == far:
            size = cut
            if step == -1:
                low, sem = low + cut, 0
        shift = step * rows if slot or step == 1 else (ring - 1) * rows
        lanes = pl.ds(p * wide, wide)
        return rcopy(
            qdo.at[pl.ds(low, size), lanes], qdo.at[pl.ds(low + shift, size), lanes],
            q_s.at[p * ring + sem], q_r.at[p * ring + sem], peer(0, step, 0),
        )

    def q_step(k, p):
        for slot, step in ((k, 1), ((ring - k) % ring, -1)):
            if k:
                q_send((slot - step) % ring, step, p).wait_recv()
            q_send(slot, step, p).start()

    def q_last(p):
        q_send(far - 1, 1, p).wait_recv()
        q_send(far + 1, -1, p).wait_recv()

    a_cp = {}
    for d in order:
        a_cp[d] = rcopy(
            kvh.at[0, pl.ds(0, rows)], kvh.at[0, pl.ds(d * rows, rows)],
            a_s.at[d], a_r.at[d], peer(0, d, 0),
        )
        a_cp[d].start()
    c_y = rcopy(kvc.at[0], kvc.at[2], i_s.at[0], i_r.at[0], peer(1, 0, 0))
    c_y.start()
    c_c = rcopy(kvc.at[0], kvc.at[1], i_s.at[1], i_r.at[1], peer(0, 0, 1))
    c_c.start()
    q_step(0, 0)
    q_step(0, 1)

    lane = lax.broadcasted_iota(jnp.int32, (1, cells), 1)
    for a in range(2):
        for d in range(ring):
            y = (pos_y + a) % 2
            z = (pos_z - d + ring) % ring
            block = (y * ring + z) * 2 * rows // BLOCK
            low = jnp.where(mask_ref[0, block] > 0, 0.0, HIDDEN)
            high = jnp.where(mask_ref[1, block] > 0, 0.0, HIDDEN)
            row = jnp.where(lane < BLOCK, low, high)
            bias_s[a, d * rows : (d + 1) * rows, :] = jnp.broadcast_to(row, (rows, cells))
    acc_h[...] = jnp.zeros_like(acc_h)
    acc_c[...] = jnp.zeros_like(acc_c)

    def column(h):
        return pl.ds(pl.multiple_of(h * HD, HD), HD)

    e_c, dp_c = (e_0, e_1), (dp_0, dp_1)

    def cell_blocks(n, hooks):
        base = cells + (n - 1) * lines if n else 0
        size = lines if n else cells
        part = slice(base, base + size)

        def raw(odd, j):
            h = 2 * j + odd
            keys = kvh[n - 1, :, 0:HD] if n else kvc[0, 0:cells, 0:HD]
            values = kvh[n - 1, :, HD : 2 * HD] if n else kvc[0, 0:cells, HD : 2 * HD]
            e_c[odd][j, part, :] = dot_nt(keys, qc[:, column(h)])
            dp_c[odd][j, part, :] = dot_nt(values, doc[:, column(h)])

        def settle(odd, j):
            h = 2 * j + odd
            s = e_c[odd][j, part, :] * factor
            if n:
                s = s + bias_s[(n - 1) // 2]
            m2 = jnp.max(fold_max(s), axis=0, keepdims=True)
            e = jnp.exp2(s - m2)
            e_c[odd][j, part, :] = e
            s_c[h, n : n + 1, :] = m2
            s_c[h, n + 8 : n + 9, :] = jnp.sum(fold_sum(e), axis=0, keepdims=True)
            inner = jnp.sum(fold_sum(e * dp_c[odd][j, part, :]), axis=0, keepdims=True)
            s_c[h, n + 16 : n + 17, :] = inner

        def body(j, carry):
            for at, step in hooks:

                @pl.when(j == at)
                def _():
                    q_step(*step)

            raw(1, j)
            settle(0, j)
            raw(0, j + 1)
            settle(1, j)
            return carry

        raw(0, 0)
        lax.fori_loop(0, half - 1, body, 0)
        raw(1, half - 1)
        settle(0, half - 1)
        settle(1, half - 1)

    for cp in moves[-2:]:
        cp.wait()
    cell_blocks(0, ())
    ktc[0] = turned(kvc[0, :, 0:HD])
    for d in order:
        a_cp[d].wait_recv()
    h_y = rcopy(kvh.at[0], kvh.at[2], i_s.at[3], i_r.at[3], peer(1, 0, 0))
    h_y.start()
    h_c = rcopy(kvh.at[0], kvh.at[1], i_s.at[4], i_r.at[4], peer(0, 0, 1))
    h_c.start()
    c_y.wait_recv()
    c_f = rcopy(kvc.at[2], kvc.at[3], i_s.at[2], i_r.at[2], peer(0, 0, 1))
    c_f.start()
    cell_blocks(1, ())
    h_c.wait_recv()
    cell_blocks(2, ((1, (1, 0)),))
    q_step(1, 1)
    kth[0] = turned(kvh[0, :, 0:HD])
    kth[1] = turned(kvh[1, :, 0:HD])
    c_c.wait_recv()
    ktc[1] = turned(kvc[1, :, 0:HD])
    ktc[2] = turned(kvc[2, :, 0:HD])
    c_f.wait_recv()
    ktc[3] = turned(kvc[3, :, 0:HD])
    h_y.wait_recv()
    h_f = rcopy(kvh.at[2], kvh.at[3], i_s.at[5], i_r.at[5], peer(0, 0, 1))
    h_f.start()
    kth[2] = turned(kvh[2, :, 0:HD])
    cell_blocks(3, ((2, (2, 0)),))
    h_f.wait_recv()
    cell_blocks(4, ((1, (2, 1)),))
    kth[3] = turned(kvh[3, :, 0:HD])

    def cell_grads(h, carry):
        for at, step in ((1, (3, 0)), (2, (3, 1))):

            @pl.when(h == at)
            def _():
                q_step(*step)

        q = [qc[:, column(2 * h + odd)] for odd in range(2)]
        g = [doc[:, column(2 * h + odd)] for odd in range(2)]
        lift, delta, dq = [], [], [None, None]
        for odd in range(2):
            tops = s_c[2 * h + odd, 0:5, :]
            best = jnp.max(tops, axis=0, keepdims=True)
            up = jnp.exp2(tops - best)
            total = jnp.sum(s_c[2 * h + odd, 8:13, :] * up, axis=0, keepdims=True)
            inner = jnp.sum(s_c[2 * h + odd, 16:21, :] * up, axis=0, keepdims=True)
            inv = 1.0 / total
            delta.append(inner * inv)
            lift.append(up * inv)
        for n in range(5):
            part = slice(cells + (n - 1) * lines, cells + n * lines) if n else slice(0, cells)
            turn = kth[n - 1] if n else ktc[0, :, 0:cells]
            dk, dv = 0.0, 0.0
            for odd in range(2):
                w = e_c[odd][h, part, :] * lift[odd][n : n + 1]
                ds = (w * (dp_c[odd][h, part, :] - delta[odd])).astype(BF16)
                dk = dk + dot_nn(ds, q[odd])
                dv = dv + dot_nn(w.astype(BF16), g[odd])
                more = dot_nn(turn, ds)
                dq[odd] = more if n == 0 else dq[odd] + more
            if n:
                acc_h[n - 1, :, 0:HD] += dk
                acc_h[n - 1, :, HD : 2 * HD] += dv
            else:
                acc_c[0, 0:cells, 0:HD] += dk
                acc_c[0, 0:cells, HD : 2 * HD] += dv
        for odd in range(2):
            dqc[:, column(2 * h + odd)] = (jnp.transpose(dq[odd]) * scale).astype(BF16)
        return carry

    lax.fori_loop(0, half, cell_grads, 0)

    dqc_cp = pltpu.make_async_copy(dqc, dqc_o, in_s.at[12])
    dqc_cp.start()
    hx_cp = []
    for a in (1, 0):
        cp = rcopy(acc_h.at[2 * a + 1], xh_r.at[a], i_s.at[6 + a], i_r.at[6 + a], peer(0, 0, 1))
        cp.start()
        hx_cp.append(cp)

    hy_cp = rcopy(yh_s, yh_r, i_s.at[8], i_r.at[8], peer(1, 0, 0))

    def grouped(p, h):
        return (
            qdo[:, pl.ds(pl.multiple_of((p * heads + h) * HD, HD), HD)],
            qdo[:, pl.ds(pl.multiple_of((p * heads + half + h) * HD, HD), HD)],
        )

    def head_stats(p, h, carry):
        q, g = grouped(p, h)
        tops, totals, inners = [], [], []
        for ab in range(4):
            s = dot_nt(kvc[ab, :, 0:HD], q)
            dp = dot_nt(kvc[ab, :, HD : 2 * HD], g)
            m2 = jnp.max(fold_max(s), axis=0, keepdims=True) * factor
            e = jnp.exp2(s * factor - m2)
            e_h[p * half + h, ab * ext : (ab + 1) * ext, :] = e
            dp_h[p * half + h, ab * ext : (ab + 1) * ext, :] = dp
            m_h[p * half + h, ab : ab + 1, :] = m2
            tops.append(m2)
            totals.append(jnp.sum(fold_sum(e), axis=0, keepdims=True))
            inners.append(jnp.sum(fold_sum(e * dp), axis=0, keepdims=True))
        best = jnp.maximum(jnp.maximum(tops[0], tops[1]), jnp.maximum(tops[2], tops[3]))
        total = jnp.zeros_like(best)
        inner = jnp.zeros_like(best)
        for ab in range(4):
            lift = jnp.exp2(tops[ab] - best)
            total = total + totals[ab] * lift
            inner = inner + inners[ab] * lift
        st[p, 0, pl.ds(h, 1), :] = best + jnp.log(total) * LOG2E
        st[p, 0, pl.ds(half + h, 1), :] = inner / total
        return carry

    t_cp = {}
    for p in range(2):
        q_last(p)

        def body(h, carry):
            if p == 0:

                @pl.when(h == half - 1)
                def _():
                    hx_cp[0].wait_recv()
                    yh_s[...] = (acc_h[2] + xh_r[1]).astype(BF16)
                    hy_cp.start()

            return head_stats(p, h, carry)

        lax.fori_loop(0, half, body, 0)
        for d in order:
            t_cp[p, d] = rcopy(
                st.at[p, 0], st.at[p, d], t_s.at[p * ring + d], t_r.at[p * ring + d],
                peer(0, d, 0),
            )
            t_cp[p, d].start()

    def merge(p):
        for d in order:
            t_cp[p, d].wait_recv()
        seen = [st[p, 0]]
        for d in range(1, ring):
            seen.append(pltpu.roll(st[p, d], d * rows, 1))
        best = seen[0][0:half]
        for d in range(1, ring):
            best = jnp.maximum(best, seen[d][0:half])
        total = jnp.zeros_like(best)
        inner = jnp.zeros_like(best)
        for d in range(ring):
            lift = jnp.exp2(seen[d][0:half] - best)
            total = total + lift
            inner = inner + seen[d][half : 2 * half] * lift
        st_f[p, 0:half] = best + jnp.log(total) * LOG2E
        st_d[p, 0:half] = inner / total

    near = 2
    first = (far, 0, near + 1, ring - near - 1, 1, ring - 1)

    def dq_send(key, p, lanes):
        low, size, slot = 0, rows, key
        if key in (1, ring - 1):
            step = -1 if key == 1 else 1
            target = dq_r.at[0 if key == 1 else 1]
        elif key in (near + 1, ring - near - 1):
            step = -1 if key == near + 1 else 1
            target = dq_x.at[0 if key == near + 1 else 1]
        elif key in (far, 0):
            step = -near if key == far else near
            slot, size, low = far, cut, 0 if key == far else cut
            target = dq_x.at[2]
        else:
            step = -near if key == near else near
            target = dq_r.at[2 if key == near else 3]
        if key in (near, ring - near):
            source = dq_m.at[0 if key == near else 1, pl.ds(0, rows), lanes]
        else:
            source = dqp.at[pl.ds(slot * rows + low, size), lanes]
        return rcopy(
            source, target.at[pl.ds(low, size), lanes],
            d_s.at[p * ring + key], d_r.at[p * ring + key], peer(0, step, 0),
        )

    def lanes_of(p):
        return pl.ds(p * side, side)

    def combine(p):
        lanes = lanes_of(p)
        for key in (far, 0, near + 1, ring - near - 1):
            dq_send(key, p, lanes).wait_recv()
        for n in range(2):
            own = dq_own[1 + n, :, lanes] + dq_x[n, :, lanes].astype(F32)
            part = slice(n * cut, (n + 1) * cut)
            rest = slice((1 - n) * cut, (2 - n) * cut)
            dq_m[n, part, lanes] = (own[part] + dq_x[2, part, lanes].astype(F32)).astype(BF16)
            dq_m[n, rest, lanes] = own[rest].astype(BF16)
        for key in (near, ring - near):
            dq_send(key, p, lanes).start()

    def head_grads(p, h, carry):
        at = p * half + 2 * h
        both = pl.ds(pl.multiple_of(at * HD, 2 * HD), 2 * HD)
        qg = [grouped(p, 2 * h + odd) for odd in range(2)]
        lift, delta, dq = [], [], [None, None]
        for odd in range(2):
            lift.append(jnp.exp2(m_h[at + odd, 0:4, :] - st_f[p, pl.ds(2 * h + odd, 1), :]))
            delta.append(st_d[p, pl.ds(2 * h + odd, 1), :])
        for ab in range(4):
            part = slice(ab * ext, (ab + 1) * ext)
            dk, dv = 0.0, 0.0
            for odd in range(2):
                w = e_h[at + odd, part, :] * lift[odd][ab : ab + 1]
                ds = (w * (dp_h[at + odd, part, :] - delta[odd])).astype(BF16)
                dk = dk + dot_nn(ds, qg[odd][0])
                dv = dv + dot_nn(w.astype(BF16), qg[odd][1])
                more = dot_nn(ktc[ab], ds)
                dq[odd] = more if ab == 0 else dq[odd] + more
            acc_c[ab, :, 0:HD] += dk
            acc_c[ab, :, HD : 2 * HD] += dv
        for odd in range(2):
            flat = jnp.transpose(dq[odd]) * scale
            for n, slot in enumerate((0, near, ring - near)):
                dq_own[n, :, column(at + odd)] = flat[slot * rows : (slot + 1) * rows]
            dqp[:, column(at + odd)] = flat.astype(BF16)
        for key in first:
            dq_send(key, p, both).start()
        return carry

    hx_cp[1].wait_recv()
    own_h = acc_h[0] + xh_r[0]
    hy_cp.wait_recv()
    own_h = own_h + yh_r[...].astype(F32)
    acc_h[0, 0:rows] = own_h[0:rows]
    zh_s[...] = own_h.astype(BF16)
    z_cp = {}
    for d in order:
        z_cp[d] = rcopy(
            zh_s.at[pl.ds(d * rows, rows)], zh_r.at[d], z_s.at[d], z_r.at[d], peer(0, -d, 0)
        )
        z_cp[d].start()

    merge(0)
    lax.fori_loop(0, half // 2, partial(head_grads, 0), 0)
    merge(1)
    lax.fori_loop(0, half // 2, partial(head_grads, 1), 0)

    cx_cp = []
    for a in (1, 0):
        cp = rcopy(acc_c.at[2 * a + 1], xc_r.at[a], i_s.at[9 + a], i_r.at[9 + a], peer(0, 0, 1))
        cp.start()
        cx_cp.append(cp)
    combine(0)
    cx_cp[0].wait_recv()
    yc_s[...] = (acc_c[2] + xc_r[1]).astype(BF16)
    cy_cp = rcopy(yc_s, yc_r, i_s.at[11], i_r.at[11], peer(1, 0, 0))
    cy_cp.start()

    combine(1)
    cx_cp[1].wait_recv()
    acc_c[0] = acc_c[0] + xc_r[0]

    d_cp = {}
    for p in range(2):
        for key in range(ring):
            d_cp[p, key] = dq_send(key, p, lanes_of(p))
        for key in (1, ring - 1, near, ring - near):
            d_cp[p, key].wait_recv()
    dq = dq_own[0]
    for n in range(4):
        dq = dq + dq_r[n].astype(F32)
    dqh_o[...] = dq.astype(BF16)

    for d in order:
        z_cp[d].wait_recv()
    own_h = acc_h[0, 0:rows]
    for d in range(1, ring):
        own_h = own_h + zh_r[d].astype(F32)
    cy_cp.wait_recv()
    own_c = acc_c[0] + yc_r[...].astype(F32)
    dkc_o[...] = (own_c[0:cells, 0:HD] * scale).astype(BF16)
    dvc_o[...] = own_c[0:cells, HD : 2 * HD].astype(BF16)
    own_h = own_h + own_c[cells:ext]
    dkh_o[...] = (own_h[:, 0:HD] * scale).astype(BF16)
    dvh_o[...] = own_h[:, HD : 2 * HD].astype(BF16)

    dqc_cp.wait()
    for group in (a_cp, z_cp, d_cp, t_cp):
        for cp in group.values():
            cp.wait_send()
    for p in range(2):
        for k in range(far):
            q_send(k, 1, p).wait_send()
            q_send((ring - k) % ring, -1, p).wait_send()
    for cp in [c_y, c_c, c_f, h_y, h_c, h_f, hy_cp, cy_cp] + hx_cp + cx_cp:
        cp.wait_send()


def put_out(*refs):
    count = len(refs) // 2
    sems = refs[-1]
    copies = [
        pltpu.make_async_copy(refs[i], refs[count + i], sems.at[i]) for i in range(count)
    ]
    for cp in copies:
        cp.start()
    for cp in copies:
        cp.wait()


def per_device(ring, q_cells, k_cells, v_cells, do_cells, q_head, k_head, v_head, do_head, vis_mask):
    cells = q_cells.shape[0]
    rows = q_head.shape[0]
    wide = q_cells.shape[1]
    heads = wide // HD
    lines = ring * rows
    half = heads // 2
    ext = cells + rows
    vmem = pl.BlockSpec(memory_space=pltpu.VMEM)
    anywhere = pl.BlockSpec(memory_space=pl.ANY)
    dma = pltpu.SemaphoreType.DMA
    results = pl.pallas_call(
        partial(kernel, ring),
        out_shape=[
            jax.ShapeDtypeStruct((cells, wide), BF16),
            jax.ShapeDtypeStruct((cells, HD), BF16),
            jax.ShapeDtypeStruct((cells, HD), BF16),
            jax.ShapeDtypeStruct((rows, wide), BF16),
            jax.ShapeDtypeStruct((rows, HD), BF16),
            jax.ShapeDtypeStruct((rows, HD), BF16),
        ],
        in_specs=[pl.BlockSpec(memory_space=pltpu.SMEM)] + [anywhere] * 8,
        out_specs=[anywhere] + [vmem] * 5,
        scratch_shapes=[
            pltpu.VMEM((cells, wide), BF16),
            pltpu.VMEM((cells, wide), BF16),
            pltpu.VMEM((cells, wide), BF16),
            dma((13,)),
            pltpu.VMEM((4, ext, 2 * HD), BF16),
            pltpu.VMEM((4, lines, 2 * HD), BF16),
            pltpu.VMEM((lines, 2 * wide), BF16),
            pltpu.VMEM((4, HD, ext), BF16),
            pltpu.VMEM((4, HD, lines), BF16),
            pltpu.VMEM((2, lines, cells), F32),
            pltpu.VMEM((half, cells + 4 * lines, cells), F32),
            pltpu.VMEM((half, cells + 4 * lines, cells), F32),
            pltpu.VMEM((half, cells + 4 * lines, cells), F32),
            pltpu.VMEM((half, cells + 4 * lines, cells), F32),
            pltpu.VMEM((heads, 24, cells), F32),
            pltpu.VMEM((heads, 4 * ext, lines), F32),
            pltpu.VMEM((heads, 4 * ext, lines), F32),
            pltpu.VMEM((heads, 8, lines), F32),
            pltpu.VMEM((2, ring, 2 * half, lines), F32),
            pltpu.VMEM((2, 8, lines), F32),
            pltpu.VMEM((2, 8, lines), F32),
            pltpu.VMEM((4, lines, 2 * HD), F32),
            pltpu.VMEM((4, ext, 2 * HD), F32),
            pltpu.VMEM((lines, wide), BF16),
            pltpu.VMEM((3, rows, wide), F32),
            pltpu.VMEM((4, rows, wide), BF16),
            pltpu.VMEM((3, rows, wide), BF16),
            pltpu.VMEM((2, rows, wide), BF16),
            pltpu.VMEM((2, lines, 2 * HD), F32),
            pltpu.VMEM((2, ext, 2 * HD), F32),
            pltpu.VMEM((lines, 2 * HD), BF16),
            pltpu.VMEM((lines, 2 * HD), BF16),
            pltpu.VMEM((ext, 2 * HD), BF16),
            pltpu.VMEM((ext, 2 * HD), BF16),
            pltpu.VMEM((lines, 2 * HD), BF16),
            pltpu.VMEM((ring, rows, 2 * HD), BF16),
        ]
        + [dma((ring,))] * 2
        + [dma((2 * ring,))] * 6
        + [dma((ring,))] * 2
        + [dma((12,))] * 2,
        compiler_params=pltpu.CompilerParams(
            collective_id=0, has_side_effects=True, vmem_limit_bytes=60 * 1024 * 1024
        ),
    )(vis_mask, q_cells, k_cells, v_cells, do_cells, q_head, k_head, v_head, do_head)
    return pl.pallas_call(
        put_out,
        out_shape=[jax.ShapeDtypeStruct(r.shape, r.dtype) for r in results],
        in_specs=[anywhere] * len(results),
        out_specs=[vmem] * len(results),
        scratch_shapes=[dma((len(results),))],
    )(*results)


def solution(mesh):
    both = P("seq", "head")
    return jax.shard_map(
        partial(per_device, mesh.shape["seq"] // 4),
        mesh=mesh,
        in_specs=(both,) * 8 + (P("seq", None),),
        out_specs=(both,) * 6,
        check_vma=False,
    )
```

```python
from functools import partial

import jax
import jax.numpy as jnp
from jax import lax
from jax.experimental import pallas as pl
from jax.experimental.pallas import tpu as pltpu
from jax.sharding import PartitionSpec as P

HD = 128
BLOCK = 128
LOG2E = 1.4426950408889634
HIDDEN = -1e30
MESH = pl.DeviceIdType.MESH
F32 = jnp.float32
BF16 = jnp.bfloat16


def dot_nt(a, b):
    return lax.dot_general(a, b, (((1,), (1,)), ((), ())), preferred_element_type=F32)


def dot_nn(a, b):
    return jnp.dot(a, b, preferred_element_type=F32)


def fold_max(x):
    return jnp.max(x.reshape(x.shape[0] // 8, 8, x.shape[1]), axis=0)


def fold_sum(x):
    return jnp.sum(x.reshape(x.shape[0] // 8, 8, x.shape[1]), axis=0)


def turned(x):
    return jnp.transpose(x.astype(F32)).astype(BF16)


def kernel(
    ring,
    mask_ref, qc_i, kc_i, vc_i, doc_i, qh_i, kh_i, vh_i, doh_i,
    dqc_o, dkc_o, dvc_o, dqh_o, dkh_o, dvh_o,
    qc, doc, dqc, in_s, kvc, kvh, qdo, ktc, kth, bias_s, e_0, e_1, dp_0, dp_1, s_c, e_h, dp_h, m_h, st, st_f, st_d,
    acc_h, acc_c, dqp, dq_own, dq_r, dq_x, dq_m, xh_r, xc_r, yh_s, yh_r, yc_s, yc_r, zh_s, zh_r,
    a_s, a_r, q_s, q_r, t_s, t_r, d_s, d_r, z_s, z_r, i_s, i_r,
):
    cells = qc.shape[0]
    rows = qh_i.shape[0]
    heads = qc.shape[1] // HD
    half = heads // 2
    wide = heads * HD
    ext = cells + rows
    lines = ring * rows
    scale = HD ** (-0.5)
    factor = scale * LOG2E
    me = lax.axis_index("seq")
    hx = lax.axis_index("head")
    core = me % 2
    pos_z = (me // 2) % ring
    pos_y = me // (2 * ring)

    def peer(a, d, b):
        y = (pos_y + a) % 2
        z = (pos_z + d + ring) % ring
        c = (core + b) % 2
        return ((y * ring + z) * 2 + c, hx)

    def rcopy(src, dst, send, recv, to):
        return pltpu.make_async_remote_copy(
            src_ref=src, dst_ref=dst, send_sem=send, recv_sem=recv,
            device_id=to, device_id_type=MESH,
        )

    barrier = pltpu.get_barrier_semaphore()
    for d in range(1, ring):
        pl.semaphore_signal(barrier, inc=1, device_id=peer(0, d, 0), device_id_type=MESH)
    pl.semaphore_signal(barrier, inc=1, device_id=peer(1, 0, 0), device_id_type=MESH)
    pl.semaphore_signal(barrier, inc=1, device_id=peer(0, 0, 1), device_id_type=MESH)

    side = half * HD
    moves = [
        (kh_i, kvh.at[0, pl.ds(0, rows), pl.ds(0, HD)]),
        (vh_i, kvh.at[0, pl.ds(0, rows), pl.ds(HD, HD)]),
        (kc_i, kvc.at[0, pl.ds(0, cells), pl.ds(0, HD)]),
        (vc_i, kvc.at[0, pl.ds(0, cells), pl.ds(HD, HD)]),
        (kh_i, kvc.at[0, pl.ds(cells, rows), pl.ds(0, HD)]),
        (vh_i, kvc.at[0, pl.ds(cells, rows), pl.ds(HD, HD)]),
    ]
    for p in range(2):
        part = pl.ds(p * side, side)
        moves.append((qh_i.at[:, part], qdo.at[pl.ds(0, rows), pl.ds(p * wide, side)]))
        moves.append((doh_i.at[:, part], qdo.at[pl.ds(0, rows), pl.ds(p * wide + side, side)]))
    moves += [(qc_i, qc), (doc_i, doc)]
    moves = [pltpu.make_async_copy(x, y, in_s.at[n]) for n, (x, y) in enumerate(moves)]
    for cp in moves:
        cp.start()
    for cp in moves[:-2]:
        cp.wait()

    pl.semaphore_wait(barrier, ring + 1)

    order = []
    for d in range(1, ring // 2 + 1):
        order.append(d)
        if ring - d != d:
            order.append(ring - d)

    far = ring // 2
    cut = rows // 2

    def q_send(slot, step, p):
        to = (slot + step) % ring
        low, size, sem = slot * rows, rows, to
        if to == far:
            size = cut
            if step == -1:
                low, sem = low + cut, 0
        shift = step * rows if slot or step == 1 else (ring - 1) * rows
        lanes = pl.ds(p * wide, wide)
        return rcopy(
            qdo.at[pl.ds(low, size), lanes], qdo.at[pl.ds(low + shift, size), lanes],
            q_s.at[p * ring + sem], q_r.at[p * ring + sem], peer(0, step, 0),
        )

    def q_step(k, p):
        for slot, step in ((k, 1), ((ring - k) % ring, -1)):
            if k:
                q_send((slot - step) % ring, step, p).wait_recv()
            q_send(slot, step, p).start()

    def q_last(p):
        q_send(far - 1, 1, p).wait_recv()
        q_send(far + 1, -1, p).wait_recv()

    a_cp = {}
    for d in order:
        a_cp[d] = rcopy(
            kvh.at[0, pl.ds(0, rows)], kvh.at[0, pl.ds(d * rows, rows)],
            a_s.at[d], a_r.at[d], peer(0, d, 0),
        )
        a_cp[d].start()
    c_y = rcopy(kvc.at[0], kvc.at[2], i_s.at[0], i_r.at[0], peer(1, 0, 0))
    c_y.start()
    c_c = rcopy(kvc.at[0], kvc.at[1], i_s.at[1], i_r.at[1], peer(0, 0, 1))
    c_c.start()
    q_step(0, 0)
    q_step(0, 1)

    lane = lax.broadcasted_iota(jnp.int32, (1, cells), 1)
    for a in range(2):
        for d in range(ring):
            y = (pos_y + a) % 2
            z = (pos_z - d + ring) % ring
            block = (y * ring + z) * 2 * rows // BLOCK
            low = jnp.where(mask_ref[0, block] > 0, 0.0, HIDDEN)
            high = jnp.where(mask_ref[1, block] > 0, 0.0, HIDDEN)
            row = jnp.where(lane < BLOCK, low, high)
            bias_s[a, d * rows : (d + 1) * rows, :] = jnp.broadcast_to(row, (rows, cells))
    acc_h[...] = jnp.zeros_like(acc_h)
    acc_c[...] = jnp.zeros_like(acc_c)

    def column(h):
        return pl.ds(pl.multiple_of(h * HD, HD), HD)

    e_c, dp_c = (e_0, e_1), (dp_0, dp_1)

    def cell_blocks(n, hooks):
        base = cells + (n - 1) * lines if n else 0
        size = lines if n else cells
        part = slice(base, base + size)

        def raw(odd, j):
            h = 2 * j + odd
            keys = kvh[n - 1, :, 0:HD] if n else kvc[0, 0:cells, 0:HD]
            values = kvh[n - 1, :, HD : 2 * HD] if n else kvc[0, 0:cells, HD : 2 * HD]
            e_c[odd][j, part, :] = dot_nt(keys, qc[:, column(h)])
            dp_c[odd][j, part, :] = dot_nt(values, doc[:, column(h)])

        def settle(odd, j):
            h = 2 * j + odd
            s = e_c[odd][j, part, :] * factor
            if n:
                s = s + bias_s[(n - 1) // 2]
            m2 = jnp.max(fold_max(s), axis=0, keepdims=True)
            e = jnp.exp2(s - m2)
            e_c[odd][j, part, :] = e
            s_c[h, n : n + 1, :] = m2
            s_c[h, n + 8 : n + 9, :] = jnp.sum(fold_sum(e), axis=0, keepdims=True)
            inner = jnp.sum(fold_sum(e * dp_c[odd][j, part, :]), axis=0, keepdims=True)
            s_c[h, n + 16 : n + 17, :] = inner

        def body(j, carry):
            for at, step in hooks:

                @pl.when(j == at)
                def _():
                    q_step(*step)

            raw(1, j)
            settle(0, j)
            raw(0, j + 1)
            settle(1, j)
            return carry

        raw(0, 0)
        lax.fori_loop(0, half - 1, body, 0)
        raw(1, half - 1)
        settle(0, half - 1)
        settle(1, half - 1)

    for cp in moves[-2:]:
        cp.wait()
    cell_blocks(0, ())
    ktc[0] = turned(kvc[0, :, 0:HD])
    for d in order:
        a_cp[d].wait_recv()
    h_y = rcopy(kvh.at[0], kvh.at[2], i_s.at[3], i_r.at[3], peer(1, 0, 0))
    h_y.start()
    h_c = rcopy(kvh.at[0], kvh.at[1], i_s.at[4], i_r.at[4], peer(0, 0, 1))
    h_c.start()
    c_y.wait_recv()
    c_f = rcopy(kvc.at[2], kvc.at[3], i_s.at[2], i_r.at[2], peer(0, 0, 1))
    c_f.start()
    cell_blocks(1, ())
    h_c.wait_recv()
    cell_blocks(2, ((1, (1, 0)),))
    q_step(1, 1)
    kth[0] = turned(kvh[0, :, 0:HD])
    kth[1] = turned(kvh[1, :, 0:HD])
    c_c.wait_recv()
    ktc[1] = turned(kvc[1, :, 0:HD])
    ktc[2] = turned(kvc[2, :, 0:HD])
    c_f.wait_recv()
    ktc[3] = turned(kvc[3, :, 0:HD])
    h_y.wait_recv()
    h_f = rcopy(kvh.at[2], kvh.at[3], i_s.at[5], i_r.at[5], peer(0, 0, 1))
    h_f.start()
    kth[2] = turned(kvh[2, :, 0:HD])
    cell_blocks(3, ((2, (2, 0)),))
    h_f.wait_recv()
    cell_blocks(4, ((1, (2, 1)),))
    kth[3] = turned(kvh[3, :, 0:HD])

    def cell_grads(h, carry):
        for at, step in ((1, (3, 0)), (2, (3, 1))):

            @pl.when(h == at)
            def _():
                q_step(*step)

        q = [qc[:, column(2 * h + odd)] for odd in range(2)]
        g = [doc[:, column(2 * h + odd)] for odd in range(2)]
        lift, delta, dq = [], [], [None, None]
        for odd in range(2):
            tops = s_c[2 * h + odd, 0:5, :]
            best = jnp.max(tops, axis=0, keepdims=True)
            up = jnp.exp2(tops - best)
            total = jnp.sum(s_c[2 * h + odd, 8:13, :] * up, axis=0, keepdims=True)
            inner = jnp.sum(s_c[2 * h + odd, 16:21, :] * up, axis=0, keepdims=True)
            inv = 1.0 / total
            delta.append(inner * inv)
            lift.append(up * inv)
        for n in range(5):
            part = slice(cells + (n - 1) * lines, cells + n * lines) if n else slice(0, cells)
            turn = kth[n - 1] if n else ktc[0, :, 0:cells]
            dk, dv = 0.0, 0.0
            for odd in range(2):
                w = e_c[odd][h, part, :] * lift[odd][n : n + 1]
                ds = (w * (dp_c[odd][h, part, :] - delta[odd])).astype(BF16)
                dk = dk + dot_nn(ds, q[odd])
                dv = dv + dot_nn(w.astype(BF16), g[odd])
                more = dot_nn(turn, ds)
                dq[odd] = more if n == 0 else dq[odd] + more
            if n:
                acc_h[n - 1, :, 0:HD] += dk
                acc_h[n - 1, :, HD : 2 * HD] += dv
            else:
                acc_c[0, 0:cells, 0:HD] += dk
                acc_c[0, 0:cells, HD : 2 * HD] += dv
        for odd in range(2):
            dqc[:, column(2 * h + odd)] = (jnp.transpose(dq[odd]) * scale).astype(BF16)
        return carry

    lax.fori_loop(0, half, cell_grads, 0)

    dqc_cp = pltpu.make_async_copy(dqc, dqc_o, in_s.at[12])
    dqc_cp.start()
    hx_cp = []
    for a in (1, 0):
        cp = rcopy(acc_h.at[2 * a + 1], xh_r.at[a], i_s.at[6 + a], i_r.at[6 + a], peer(0, 0, 1))
        cp.start()
        hx_cp.append(cp)

    hy_cp = rcopy(yh_s, yh_r, i_s.at[8], i_r.at[8], peer(1, 0, 0))

    def grouped(p, h):
        return (
            qdo[:, pl.ds(pl.multiple_of((p * heads + h) * HD, HD), HD)],
            qdo[:, pl.ds(pl.multiple_of((p * heads + half + h) * HD, HD), HD)],
        )

    def head_stats(p, h, carry):
        q, g = grouped(p, h)
        tops, totals, inners = [], [], []
        for ab in range(4):
            s = dot_nt(kvc[ab, :, 0:HD], q)
            dp = dot_nt(kvc[ab, :, HD : 2 * HD], g)
            m2 = jnp.max(fold_max(s), axis=0, keepdims=True) * factor
            e = jnp.exp2(s * factor - m2)
            e_h[p * half + h, ab * ext : (ab + 1) * ext, :] = e
            dp_h[p * half + h, ab * ext : (ab + 1) * ext, :] = dp
            m_h[p * half + h, ab : ab + 1, :] = m2
            tops.append(m2)
            totals.append(jnp.sum(fold_sum(e), axis=0, keepdims=True))
            inners.append(jnp.sum(fold_sum(e * dp), axis=0, keepdims=True))
        best = jnp.maximum(jnp.maximum(tops[0], tops[1]), jnp.maximum(tops[2], tops[3]))
        total = jnp.zeros_like(best)
        inner = jnp.zeros_like(best)
        for ab in range(4):
            lift = jnp.exp2(tops[ab] - best)
            total = total + totals[ab] * lift
            inner = inner + inners[ab] * lift
        st[p, 0, pl.ds(h, 1), :] = best + jnp.log(total) * LOG2E
        st[p, 0, pl.ds(half + h, 1), :] = inner / total
        return carry

    t_cp = {}
    for p in range(2):
        q_last(p)

        def body(h, carry):
            if p == 0:

                @pl.when(h == half - 1)
                def _():
                    hx_cp[0].wait_recv()
                    yh_s[...] = (acc_h[2] + xh_r[1]).astype(BF16)
                    hy_cp.start()

            return head_stats(p, h, carry)

        lax.fori_loop(0, half, body, 0)
        for d in order:
            t_cp[p, d] = rcopy(
                st.at[p, 0], st.at[p, d], t_s.at[p * ring + d], t_r.at[p * ring + d],
                peer(0, d, 0),
            )
            t_cp[p, d].start()

    def merge(p):
        for d in order:
            t_cp[p, d].wait_recv()
        seen = [st[p, 0]]
        for d in range(1, ring):
            seen.append(pltpu.roll(st[p, d], d * rows, 1))
        best = seen[0][0:half]
        for d in range(1, ring):
            best = jnp.maximum(best, seen[d][0:half])
        total = jnp.zeros_like(best)
        inner = jnp.zeros_like(best)
        for d in range(ring):
            lift = jnp.exp2(seen[d][0:half] - best)
            total = total + lift
            inner = inner + seen[d][half : 2 * half] * lift
        st_f[p, 0:half] = best + jnp.log(total) * LOG2E
        st_d[p, 0:half] = inner / total

    near = 2
    first = (far, 0, near + 1, ring - near - 1, 1, ring - 1)

    def dq_send(key, p, lanes):
        low, size, slot = 0, rows, key
        if key in (1, ring - 1):
            step = -1 if key == 1 else 1
            target = dq_r.at[0 if key == 1 else 1]
        elif key in (near + 1, ring - near - 1):
            step = -1 if key == near + 1 else 1
            target = dq_x.at[0 if key == near + 1 else 1]
        elif key in (far, 0):
            step = -near if key == far else near
            slot, size, low = far, cut, 0 if key == far else cut
            target = dq_x.at[2]
        else:
            step = -near if key == near else near
            target = dq_r.at[2 if key == near else 3]
        if key in (near, ring - near):
            source = dq_m.at[0 if key == near else 1, pl.ds(0, rows), lanes]
        else:
            source = dqp.at[pl.ds(slot * rows + low, size), lanes]
        return rcopy(
            source, target.at[pl.ds(low, size), lanes],
            d_s.at[p * ring + key], d_r.at[p * ring + key], peer(0, step, 0),
        )

    def lanes_of(p):
        return pl.ds(p * side, side)

    def combine(p):
        lanes = lanes_of(p)
        for key in (far, 0, near + 1, ring - near - 1):
            dq_send(key, p, lanes).wait_recv()
        for n in range(2):
            own = dq_own[1 + n, :, lanes] + dq_x[n, :, lanes].astype(F32)
            part = slice(n * cut, (n + 1) * cut)
            rest = slice((1 - n) * cut, (2 - n) * cut)
            dq_m[n, part, lanes] = (own[part] + dq_x[2, part, lanes].astype(F32)).astype(BF16)
            dq_m[n, rest, lanes] = own[rest].astype(BF16)
        for key in (near, ring - near):
            dq_send(key, p, lanes).start()

    cx_cp = [
        rcopy(acc_c.at[2 * a + 1], xc_r.at[a], i_s.at[9 + a], i_r.at[9 + a], peer(0, 0, 1))
        for a in (1, 0)
    ]

    def head_grads(p, h, carry):
        at = p * half + 2 * h
        both = pl.ds(pl.multiple_of(at * HD, 2 * HD), 2 * HD)
        qg = [grouped(p, 2 * h + odd) for odd in range(2)]
        lift, delta, dq = [], [], [None, None]
        for odd in range(2):
            lift.append(jnp.exp2(m_h[at + odd, 0:4, :] - st_f[p, pl.ds(2 * h + odd, 1), :]))
            delta.append(st_d[p, pl.ds(2 * h + odd, 1), :])
        for ab in (3, 2, 1, 0):
            part = slice(ab * ext, (ab + 1) * ext)
            dk, dv = 0.0, 0.0
            for odd in range(2):
                w = e_h[at + odd, part, :] * lift[odd][ab : ab + 1]
                ds = (w * (dp_h[at + odd, part, :] - delta[odd])).astype(BF16)
                dk = dk + dot_nn(ds, qg[odd][0])
                dv = dv + dot_nn(w.astype(BF16), qg[odd][1])
                more = dot_nn(ktc[ab], ds)
                dq[odd] = more if ab == 3 else dq[odd] + more
            acc_c[ab, :, 0:HD] += dk
            acc_c[ab, :, HD : 2 * HD] += dv
            if p == 1 and ab == 3:

                @pl.when(h == half // 2 - 1)
                def _():
                    cx_cp[0].start()

        for odd in range(2):
            flat = jnp.transpose(dq[odd]) * scale
            for n, slot in enumerate((0, near, ring - near)):
                dq_own[n, :, column(at + odd)] = flat[slot * rows : (slot + 1) * rows]
            dqp[:, column(at + odd)] = flat.astype(BF16)
        for key in first:
            dq_send(key, p, both).start()
        return carry

    hx_cp[1].wait_recv()
    own_h = acc_h[0] + xh_r[0]
    hy_cp.wait_recv()
    own_h = own_h + yh_r[...].astype(F32)
    acc_h[0, 0:rows] = own_h[0:rows]
    zh_s[...] = own_h.astype(BF16)
    z_cp = {}
    for d in order:
        z_cp[d] = rcopy(
            zh_s.at[pl.ds(d * rows, rows)], zh_r.at[d], z_s.at[d], z_r.at[d], peer(0, -d, 0)
        )
        z_cp[d].start()

    merge(0)
    lax.fori_loop(0, half // 2, partial(head_grads, 0), 0)
    merge(1)
    lax.fori_loop(0, half // 2, partial(head_grads, 1), 0)

    cx_cp[1].start()
    cx_cp[0].wait_recv()
    yc_s[...] = (acc_c[2] + xc_r[1]).astype(BF16)
    cy_cp = rcopy(yc_s, yc_r, i_s.at[11], i_r.at[11], peer(1, 0, 0))
    cy_cp.start()
    combine(0)

    combine(1)
    cx_cp[1].wait_recv()
    acc_c[0] = acc_c[0] + xc_r[0]

    d_cp = {}
    for p in range(2):
        for key in range(ring):
            d_cp[p, key] = dq_send(key, p, lanes_of(p))
        for key in (1, ring - 1, near, ring - near):
            d_cp[p, key].wait_recv()
    dq = dq_own[0]
    for n in range(4):
        dq = dq + dq_r[n].astype(F32)
    dqh_o[...] = dq.astype(BF16)

    for d in order:
        z_cp[d].wait_recv()
    own_h = acc_h[0, 0:rows]
    for d in range(1, ring):
        own_h = own_h + zh_r[d].astype(F32)
    cy_cp.wait_recv()
    own_c = acc_c[0] + yc_r[...].astype(F32)
    dkc_o[...] = (own_c[0:cells, 0:HD] * scale).astype(BF16)
    dvc_o[...] = own_c[0:cells, HD : 2 * HD].astype(BF16)
    own_h = own_h + own_c[cells:ext]
    dkh_o[...] = (own_h[:, 0:HD] * scale).astype(BF16)
    dvh_o[...] = own_h[:, HD : 2 * HD].astype(BF16)

    dqc_cp.wait()
    for group in (a_cp, z_cp, d_cp, t_cp):
        for cp in group.values():
            cp.wait_send()
    for p in range(2):
        for k in range(far):
            q_send(k, 1, p).wait_send()
            q_send((ring - k) % ring, -1, p).wait_send()
    for cp in [c_y, c_c, c_f, h_y, h_c, h_f, hy_cp, cy_cp] + hx_cp + cx_cp:
        cp.wait_send()


def put_out(*refs):
    count = len(refs) // 2
    sems = refs[-1]
    copies = [
        pltpu.make_async_copy(refs[i], refs[count + i], sems.at[i]) for i in range(count)
    ]
    for cp in copies:
        cp.start()
    for cp in copies:
        cp.wait()


def per_device(ring, q_cells, k_cells, v_cells, do_cells, q_head, k_head, v_head, do_head, vis_mask):
    cells = q_cells.shape[0]
    rows = q_head.shape[0]
    wide = q_cells.shape[1]
    heads = wide // HD
    lines = ring * rows
    half = heads // 2
    ext = cells + rows
    vmem = pl.BlockSpec(memory_space=pltpu.VMEM)
    anywhere = pl.BlockSpec(memory_space=pl.ANY)
    dma = pltpu.SemaphoreType.DMA
    results = pl.pallas_call(
        partial(kernel, ring),
        out_shape=[
            jax.ShapeDtypeStruct((cells, wide), BF16),
            jax.ShapeDtypeStruct((cells, HD), BF16),
            jax.ShapeDtypeStruct((cells, HD), BF16),
            jax.ShapeDtypeStruct((rows, wide), BF16),
            jax.ShapeDtypeStruct((rows, HD), BF16),
            jax.ShapeDtypeStruct((rows, HD), BF16),
        ],
        in_specs=[pl.BlockSpec(memory_space=pltpu.SMEM)] + [anywhere] * 8,
        out_specs=[anywhere] + [vmem] * 5,
        scratch_shapes=[
            pltpu.VMEM((cells, wide), BF16),
            pltpu.VMEM((cells, wide), BF16),
            pltpu.VMEM((cells, wide), BF16),
            dma((13,)),
            pltpu.VMEM((4, ext, 2 * HD), BF16),
            pltpu.VMEM((4, lines, 2 * HD), BF16),
            pltpu.VMEM((lines, 2 * wide), BF16),
            pltpu.VMEM((4, HD, ext), BF16),
            pltpu.VMEM((4, HD, lines), BF16),
            pltpu.VMEM((2, lines, cells), F32),
            pltpu.VMEM((half, cells + 4 * lines, cells), F32),
            pltpu.VMEM((half, cells + 4 * lines, cells), F32),
            pltpu.VMEM((half, cells + 4 * lines, cells), F32),
            pltpu.VMEM((half, cells + 4 * lines, cells), F32),
            pltpu.VMEM((heads, 24, cells), F32),
            pltpu.VMEM((heads, 4 * ext, lines), F32),
            pltpu.VMEM((heads, 4 * ext, lines), F32),
            pltpu.VMEM((heads, 8, lines), F32),
            pltpu.VMEM((2, ring, 2 * half, lines), F32),
            pltpu.VMEM((2, 8, lines), F32),
            pltpu.VMEM((2, 8, lines), F32),
            pltpu.VMEM((4, lines, 2 * HD), F32),
            pltpu.VMEM((4, ext, 2 * HD), F32),
            pltpu.VMEM((lines, wide), BF16),
            pltpu.VMEM((3, rows, wide), F32),
            pltpu.VMEM((4, rows, wide), BF16),
            pltpu.VMEM((3, rows, wide), BF16),
            pltpu.VMEM((2, rows, wide), BF16),
            pltpu.VMEM((2, lines, 2 * HD), F32),
            pltpu.VMEM((2, ext, 2 * HD), F32),
            pltpu.VMEM((lines, 2 * HD), BF16),
            pltpu.VMEM((lines, 2 * HD), BF16),
            pltpu.VMEM((ext, 2 * HD), BF16),
            pltpu.VMEM((ext, 2 * HD), BF16),
            pltpu.VMEM((lines, 2 * HD), BF16),
            pltpu.VMEM((ring, rows, 2 * HD), BF16),
        ]
        + [dma((ring,))] * 2
        + [dma((2 * ring,))] * 6
        + [dma((ring,))] * 2
        + [dma((12,))] * 2,
        compiler_params=pltpu.CompilerParams(
            collective_id=0, has_side_effects=True, vmem_limit_bytes=60 * 1024 * 1024
        ),
    )(vis_mask, q_cells, k_cells, v_cells, do_cells, q_head, k_head, v_head, do_head)
    return pl.pallas_call(
        put_out,
        out_shape=[jax.ShapeDtypeStruct(r.shape, r.dtype) for r in results],
        in_specs=[anywhere] * len(results),
        out_specs=[vmem] * len(results),
        scratch_shapes=[dma((len(results),))],
    )(*results)


def solution(mesh):
    both = P("seq", "head")
    return jax.shard_map(
        partial(per_device, mesh.shape["seq"] // 4),
        mesh=mesh,
        in_specs=(both,) * 8 + (P("seq", None),),
        out_specs=(both,) * 6,
        check_vma=False,
    )
```
